32 devices in a mesh: grp: 2 (over x), spec: 16 (over z, y, core).
Axes of the slice: x: 2, y: 2, z: 4, core: 2. Of those that a mesh axis runs over, the one named last changes fastest.
Arguments:
- vorticity: bfloat16 [128, 1280, 2560], P('grp', 'spec'), parts along dimension 0, may hold values from -32 to 32
- lat_order: int32 [1280], replicated, may hold values from 0 to 1279, as said below
- storm_labels: int32 [128, 256, 720], P('grp', 'spec'), parts along dimension 0, may hold values from 0 to 511, as said below
- storm_owner: int32 [512], P('grp'), parts along dimension 0, may hold values from 0 to 255, each once
Outputs:
- filtered: bfloat16 [128, 256, 720], P('grp', 'spec'), parts along dimension 0
- storm_peak: float32 [512], P(('grp', 'spec')), parts along dimension 0
The draws below stay inside these ranges and needn't reach their ends.
There are 2 independent parts, one for each index of `grp`. The reference program is written for one: setup_inputs(seed, part) draws one part's arguments, and reference() takes and returns one part's arrays. A program takes and returns all parts, laid end to end along the dimension named above; an argument that names none is the same for every part. Nothing has to cross between parts.
Inputs may be any that keep to these rules, and one draw needn't show every extreme that they name: `storm_labels`: labels 256 and above mark points outside every storm; every storm number below 256 labels at least one point of the window. Row j of vorticity lies on latitude lat_order[j], counted from the north; each latitude once. In each block of 80 rows, the second half holds the latitudes 1280 - 1 minus those of the first half, in the same order. `storm_owner`: each slot is owned by one storm.
All inputs are finite; a program needn't handle non-finite values.
Results may differ from the reference program's by a relative error of at most 0.0054.
Values may be sent and summed in bfloat16 or wider, within the bound.
No kernel may reach another device: no remote copies, remote signals or barrier semaphores. Data moves between devices by JAX's collectives and lax.ppermute only.
A program may use at most 192 MiB of HBM per device.

```python
import math
import jax
import jax.numpy as jnp
from jax import lax

F = 64
NLAT = 1280
NLON = 2560
MW = 256
OUT_LAT = 256
OUT_LON = 720
NSTORM = 256
N_SPEC = 16


def draw_lat_order(key, part):
    pair_count = NLAT // 2
    half_block = NLAT // (2 * N_SPEC)
    key_pairs = jax.random.fold_in(key, 21)
    northern = jax.random.permutation(key_pairs, jnp.arange(pair_count, dtype=jnp.int32))
    northern = northern.reshape(N_SPEC, half_block)
    southern = NLAT - 1 - northern
    return jnp.concatenate([northern, southern], axis=1).reshape(NLAT).astype(jnp.int32)


def draw_storm_labels(key, part):
    element_count = F * OUT_LAT * OUT_LON
    stride = element_count // NSTORM
    key_labels = jax.random.fold_in(key, 11)
    key_places = jax.random.fold_in(key, 12)
    labels = jax.random.randint(key_labels, (element_count,), 0, 2 * NSTORM, dtype=jnp.int32)
    offsets = jax.random.randint(key_places, (NSTORM,), 0, stride - 1, dtype=jnp.int32)
    storms = jnp.arange(NSTORM, dtype=jnp.int32)
    places = storms * stride + offsets
    labels = labels.at[places].set(storms)
    labels = labels.at[places[0] + 1].set(2 * NSTORM - 1)
    return labels.reshape(F, OUT_LAT, OUT_LON)


def block_levels(rng, shape, pieces, smallest, top_value):
    loudness = 1.0
    for axis_at, shards_of in pieces:
        draws = jax.random.uniform(jax.random.fold_in(jax.random.fold_in(rng, 6), axis_at), (shards_of,), jnp.float32, smallest / len(pieces), top_value / len(pieces))
        loudness = loudness * jnp.repeat(jnp.exp(draws), shape[axis_at] // shards_of).reshape((-1,) + (1,) * (len(shape) - 1 - axis_at))
    return loudness


def centred(own_key, dims, scale, reach, pieces=(), held_as=jnp.bfloat16):
    gain = block_levels(own_key, dims, pieces, -0.22, 0.18) if pieces else 1.0
    array = jax.random.normal(own_key, dims, jnp.float32) * scale * gain
    return jnp.minimum(jnp.maximum(array, -reach), reach).astype(held_as)


def setup_inputs(seed: int = 0, part: int = 0) -> dict:
    arg_keys = jax.random.split(jax.random.key(seed), 5)
    part_keys = jax.random.split(jax.random.fold_in(arg_keys[4], part), 5)
    return {
        "vorticity": centred(part_keys[0], (F, NLAT, NLON), 4.0, 32.0, ((1, 16),)),
        "lat_order": draw_lat_order(jax.random.fold_in(arg_keys[4], 71), part),
        "storm_labels": draw_storm_labels(jax.random.fold_in(jax.random.fold_in(arg_keys[4], part), 71), part),
        "storm_owner": jax.random.permutation(part_keys[3], NSTORM).astype(jnp.int32),
    }


HIGHEST = lax.Precision.HIGHEST
FLOOR = -1e+30

def fourier_table(wave_numbers, lon_count):
    longitudes = jnp.arange(lon_count, dtype=jnp.int32)
    phase_steps = longitudes[:, None] * wave_numbers[None, :] % lon_count
    angles = phase_steps.astype(jnp.float32) * (2.0 * math.pi / lon_count)
    stacked = jnp.stack([jnp.cos(angles), -jnp.sin(angles)], axis=-1) / lon_count
    return stacked.astype(jnp.bfloat16)

def synthesis_table(wave_numbers, lon_count):
    longitudes = jnp.arange(lon_count, dtype=jnp.int32)
    phase_steps = wave_numbers[:, None] * longitudes[None, :] % lon_count
    angles = phase_steps.astype(jnp.float32) * (2.0 * math.pi / lon_count)
    factor = jnp.where(wave_numbers == 0, 1.0, 2.0).astype(jnp.float32)[:, None]
    stacked = jnp.stack([factor * jnp.cos(angles), -factor * jnp.sin(angles)], axis=1)
    return stacked.astype(jnp.bfloat16)

def node_values(lat_order, lat_count, band_count, lon_count):
    colatitude = math.pi * (4.0 * lat_order.astype(jnp.float32) + 3.0) / (4.0 * lat_count + 2.0)
    weights = math.pi / lat_count * jnp.sin(colatitude)
    band_index = jnp.arange(band_count, dtype=jnp.float32)
    latitude = ((band_count - 1) / 2.0 - band_index) * (360.0 / lon_count) * (math.pi / 180.0)
    sine_values = jnp.concatenate([jnp.sin(colatitude), jnp.cos(latitude)])
    cosines = jnp.concatenate([jnp.cos(colatitude), jnp.sin(latitude)])
    return (sine_values, cosines, weights)

def legendre(orders, sine_values, cosines, degree_count):
    counters = jnp.arange(1, degree_count, dtype=jnp.float32)
    increments = jnp.log((2.0 * counters + 1.0) / (2.0 * counters))
    partial_value = lax.optimization_barrier(jnp.sum(jnp.where(counters[None, :] <= orders[:, None], increments[None, :], 0.0), axis=1))
    diagonal_start = jnp.exp(0.5 * math.log(0.5) + 0.5 * partial_value[:, None] + orders[:, None] * jnp.log(sine_values)[None, :])
    squared = orders * orders

    def advance(state_pair, degree):
        previous, earlier = state_pair
        degree_value = degree.astype(jnp.float32)
        first_scale = jnp.sqrt(jnp.maximum(4.0 * degree_value * degree_value - 1.0, 1.0) / jnp.maximum(degree_value * degree_value - squared, 1.0))
        shifted = (degree_value - 1.0) * (degree_value - 1.0)
        second_scale = jnp.sqrt(jnp.maximum(shifted - squared, 0.0) / jnp.maximum(4.0 * shifted - 1.0, 1.0))
        recurred = first_scale[:, None] * (cosines[None, :] * previous - second_scale[:, None] * earlier)
        current = jnp.where(degree_value < orders[:, None], 0.0, jnp.where(degree_value == orders[:, None], diagonal_start, recurred))
        return ((current, previous), current)
    zero_rows = jnp.zeros((orders.shape[0], sine_values.shape[0]), jnp.float32)
    final_state, degree_rows = lax.scan(advance, (zero_rows, zero_rows), jnp.arange(degree_count, dtype=jnp.int32), unroll=16)
    return jnp.transpose(degree_rows, (1, 0, 2))

def reference(vorticity, lat_order, storm_labels, storm_owner):
    field_count = vorticity.shape[0]
    wave_numbers = jnp.arange(MW, dtype=jnp.int32)
    forward = fourier_table(wave_numbers, NLON)
    coefficients = jnp.einsum('fjl,lqr->qjrf', vorticity.astype(jnp.float32), forward.astype(jnp.float32), precision=HIGHEST)
    coefficients = coefficients.reshape(MW, NLAT, 2 * field_count)
    sine_values, cosines, weights = node_values(lat_order, NLAT, OUT_LAT, OUT_LON)
    group_size = 8

    def per_group(group_index):
        orders = (group_index * group_size + jnp.arange(group_size, dtype=jnp.int32)).astype(jnp.float32)
        tables = legendre(orders, sine_values, cosines, MW)
        weighted = tables[:, :, :NLAT] * weights[None, None, :]
        evaluated = tables[:, :, NLAT:]
        coef_block = lax.dynamic_slice_in_dim(coefficients, (group_index * group_size).astype(jnp.int32), group_size, 0)
        spectral = jnp.einsum('knj,kjc->knc', weighted, coef_block, precision=HIGHEST)
        band_part = jnp.einsum('kno,knc->koc', evaluated, spectral, precision=HIGHEST)
        return band_part.astype(jnp.bfloat16)
    band_rows = lax.map(per_group, jnp.arange(MW // group_size, dtype=jnp.int32))
    band_rows = band_rows.reshape(MW, OUT_LAT, 2, field_count)
    synthesis = synthesis_table(wave_numbers, OUT_LON)
    grid_values = jnp.einsum('qorf,qrl->fol', band_rows.astype(jnp.float32), synthesis.astype(jnp.float32), precision=HIGHEST)
    filtered = grid_values.astype(jnp.bfloat16)
    storm_maxima = jnp.full((NSTORM,), FLOOR, grid_values.dtype).at[storm_labels.reshape(-1)].max(grid_values.reshape(-1), mode='drop')
    storm_peak = jnp.zeros((NSTORM,), grid_values.dtype).at[storm_owner].set(storm_maxima)
    return (filtered, storm_peak)
```

```python
import functools
import math

import jax
import jax.numpy as jnp
import numpy as np
from jax import lax
from jax.experimental import pallas as pl
from jax.experimental.pallas import tpu as pltpu
from jax.sharding import Mesh
from jax.sharding import PartitionSpec as P

MW = 256
OUT_LAT = 256
OUT_LON = 720
FLOOR = -1e30
CHUNKS = 2
LANES = 128


def fourier_table(lon_count):
    steps = np.arange(lon_count)[:, None] * np.arange(MW)[None, :] % lon_count
    angles = steps * (2.0 * math.pi / lon_count)
    return np.stack([np.cos(angles), -np.sin(angles)], axis=-1) / lon_count


def synthesis_table(lon_count):
    steps = np.arange(MW)[:, None] * np.arange(lon_count)[None, :] % lon_count
    angles = steps * (2.0 * math.pi / lon_count)
    factor = np.where(np.arange(MW) == 0, 1.0, 2.0)[:, None]
    return np.stack([factor * np.cos(angles), -factor * np.sin(angles)], axis=1)


def diagonal_logs():
    counters = np.arange(1, MW, dtype=np.float64)
    increments = np.log((2.0 * counters + 1.0) / (2.0 * counters))
    sums = np.concatenate([[0.0], np.cumsum(increments)])
    return (0.5 * math.log(0.5) + 0.5 * sums).astype(np.float32)


def kernel_table(orders, start, cosines, weights, out_rows):
    slots, columns = start.shape
    in_rows = columns - out_rows
    degrees = MW
    group = 8
    tiles = columns // LANES
    out_tiles = out_rows // LANES

    def body(order_ref, start_ref, cos_ref, weight_ref, out_ref, table_ref):
        m = jnp.broadcast_to(order_ref[...], (group, LANES))
        cosine = [cos_ref[0:1, t * LANES : (t + 1) * LANES] for t in range(tiles)]

        def step(k, carry):
            previous, earlier = carry
            offset = k.astype(jnp.float32)
            degree = m + offset
            below = degree - 1.0
            first = jnp.sqrt((4.0 * degree * degree - 1.0) / (offset * (2.0 * m + offset)))
            second = jnp.sqrt(
                (offset - 1.0) * (2.0 * m + offset - 1.0) / jnp.maximum(4.0 * below * below - 1.0, 1.0)
            )
            keep = degree <= degrees - 1.0
            row = pl.multiple_of(k * group, group)
            current = []
            for t in range(tiles):
                value = first * (cosine[t] * previous[t] - second * earlier[t])
                current.append(value)
                stored = jnp.where(keep, value, 0.0) if t < out_tiles else value
                table_ref[t, pl.ds(row, group), :] = stored
            return (tuple(current), previous)

        first_rows = tuple(start_ref[:, t * LANES : (t + 1) * LANES] for t in range(tiles))
        for t in range(tiles):
            table_ref[t, 0:group, :] = first_rows[t]
        zeros = tuple(jnp.zeros((group, LANES), jnp.float32) for _ in range(tiles))
        lax.fori_loop(1, degrees, step, (first_rows, zeros))
        weight = weight_ref[...]
        for s in range(group):
            values = [table_ref[t, pl.ds(s, degrees, stride=group), :] for t in range(tiles)]
            product = lax.dot_general(
                jnp.concatenate(values[:out_tiles], axis=1),
                jnp.concatenate(values[out_tiles:], axis=1),
                (((0,), (0,)), ((), ())),
                precision=lax.Precision.HIGHEST,
                preferred_element_type=jnp.float32,
            )
            out_ref[s] = (product * weight).astype(jnp.bfloat16)

    return pl.pallas_call(
        body,
        out_shape=jax.ShapeDtypeStruct((slots, out_rows, in_rows), jnp.bfloat16),
        grid=(slots // group,),
        in_specs=[
            pl.BlockSpec((group, 1), lambda g: (g, 0)),
            pl.BlockSpec((group, columns), lambda g: (g, 0)),
            pl.BlockSpec((1, columns), lambda g: (0, 0)),
            pl.BlockSpec((1, in_rows), lambda g: (0, 0)),
        ],
        out_specs=pl.BlockSpec((group, out_rows, in_rows), lambda g: (g, 0, 0)),
        scratch_shapes=[pltpu.VMEM((columns // LANES, degrees * group, LANES), jnp.float32)],
        compiler_params=pltpu.CompilerParams(vmem_limit_bytes=56 << 20),
    )(orders, start, cosines, weights)


def apply_table(table, received, slot_base):
    senders, slots, rows, columns = received.shape
    out_rows = table.shape[1]
    half = out_rows // 2

    def body(table_ref, data_ref, own_ref, other_ref):
        data = data_ref[...].reshape(senders * rows, columns)
        product = jnp.dot(table_ref[...], data, preferred_element_type=jnp.float32)
        own_ref[...] = product[:half]
        other_ref[...] = product[half:].astype(jnp.bfloat16)

    return pl.pallas_call(
        body,
        out_shape=(
            jax.ShapeDtypeStruct((slots, half, columns), jnp.float32),
            jax.ShapeDtypeStruct((slots, half, columns), jnp.bfloat16),
        ),
        grid=(slots,),
        in_specs=[
            pl.BlockSpec((None, out_rows, senders * rows), lambda s: (s + slot_base, 0, 0)),
            pl.BlockSpec((senders, None, rows, columns), lambda s: (0, s, 0, 0)),
        ],
        out_specs=(
            pl.BlockSpec((None, half, columns), lambda s: (s, 0, 0)),
            pl.BlockSpec((None, half, columns), lambda s: (s, 0, 0)),
        ),
        compiler_params=pltpu.CompilerParams(vmem_limit_bytes=56 << 20),
    )(table, received)


def storm_maxima(values, labels, storm_count):
    rows, lon_count = values.shape
    block = math.gcd(rows, 64)
    lane_starts = range(0, lon_count, LANES)

    def body(value_ref, label_ref, out_ref):
        @pl.when(pl.program_id(0) == 0)
        def _():
            out_ref[...] = jnp.full(out_ref.shape, FLOOR, jnp.float32)

        for lane in lane_starts:
            width = min(LANES, lon_count - lane)
            cells = [
                (
                    value_ref[r : r + 8, lane : lane + width],
                    label_ref[r : r + 8, lane : lane + width],
                )
                for r in range(0, block, 8)
            ]

            def per_storm(storm, carry):
                picked = [jnp.where(label == storm, value, FLOOR) for value, label in cells]
                while len(picked) > 1:
                    picked = [jnp.maximum(a, b) for a, b in zip(picked[::2], picked[1::2])]
                out_ref[storm, :, 0:width] = jnp.maximum(out_ref[storm, :, 0:width], picked[0])
                return carry

            lax.fori_loop(0, storm_count, per_storm, 0, unroll=8)

    return pl.pallas_call(
        body,
        out_shape=jax.ShapeDtypeStruct((storm_count, 8, LANES), jnp.float32),
        grid=(rows // block,),
        in_specs=[
            pl.BlockSpec((block, lon_count), lambda i: (i, 0)),
            pl.BlockSpec((block, lon_count), lambda i: (i, 0)),
        ],
        out_specs=pl.BlockSpec((storm_count, 8, LANES), lambda i: (0, 0, 0)),
        compiler_params=pltpu.CompilerParams(vmem_limit_bytes=56 << 20),
    )(values, labels)


def local(vorticity, lat_order, storm_labels, storm_owner):
    field_count, lat_rows, lon_count = vorticity.shape
    lat_count = lat_order.shape[0]
    halves = lax.axis_size("half")
    ranks = lax.axis_size("rest")
    half_index = lax.axis_index("half")
    rank = lax.axis_index("rest")
    band_rows = storm_labels.shape[1]
    storm_count = storm_owner.shape[0]
    slots = MW // ranks
    chunk_slots = slots // CHUNKS
    columns = 2 * field_count
    out_half = OUT_LAT // halves

    table = fourier_table(lon_count).reshape(lon_count, CHUNKS, chunk_slots, ranks, 2)
    table = table.transpose(1, 0, 3, 2, 4).reshape(CHUNKS, lon_count, ranks * chunk_slots, 2)
    table = table.astype(jnp.bfloat16)

    received = []
    for c in range(CHUNKS):
        coefficients = jnp.einsum(
            "fjl,lqr->qjrf", vorticity, jnp.asarray(table[c]), preferred_element_type=jnp.float32
        )
        coefficients = coefficients.astype(jnp.bfloat16).reshape(
            ranks, chunk_slots, lat_rows, columns
        )
        received.append(
            lax.all_to_all(coefficients, "rest", split_axis=0, concat_axis=0, tiled=True)
        )

    half_rows = ranks * lat_rows
    own_order = lax.dynamic_slice_in_dim(lat_order, half_index * half_rows, half_rows)
    colatitude = math.pi * (4.0 * own_order.astype(jnp.float32) + 3.0) / (4.0 * lat_count + 2.0)
    weights = math.pi / lat_count * jnp.sin(colatitude)
    band_index = jnp.arange(OUT_LAT, dtype=jnp.int32)
    band_index = ((band_index + half_index * out_half) % OUT_LAT).astype(jnp.float32)
    latitude = ((OUT_LAT - 1) / 2.0 - band_index) * (360.0 / OUT_LON) * (math.pi / 180.0)
    sine_values = jnp.concatenate([jnp.cos(latitude), jnp.sin(colatitude)])
    cosines = jnp.concatenate([jnp.sin(latitude), jnp.cos(colatitude)])
    orders = jnp.arange(slots, dtype=jnp.int32) * ranks + rank
    start_logs = jnp.asarray(diagonal_logs().reshape(slots, ranks))
    start_logs = lax.dynamic_slice_in_dim(start_logs, rank, 1, axis=1)
    orders = orders.astype(jnp.float32)[:, None]
    start = jnp.exp(start_logs + orders * jnp.log(sine_values)[None, :])
    kernel = kernel_table(orders, start, cosines[None, :], weights[None, :], OUT_LAT)

    gathered = []
    swap = [(0, 1), (1, 0)]
    for c in range(CHUNKS):
        own, other = apply_table(kernel, received[c], c * chunk_slots)
        mirrored = lax.ppermute(other, "half", swap)
        band = (own + mirrored.astype(jnp.float32)).astype(jnp.bfloat16)
        band = lax.all_to_all(band, "rest", split_axis=1, concat_axis=0, tiled=True)
        gathered.append(band.reshape(ranks, chunk_slots, band_rows, 2, field_count))

    gathered = jnp.concatenate(gathered, axis=1)
    synthesis = synthesis_table(OUT_LON).reshape(slots, ranks, 2, OUT_LON)
    synthesis = jnp.asarray(synthesis.transpose(1, 0, 2, 3).astype(jnp.bfloat16))
    grid_values = jnp.einsum(
        "qsorf,qsrl->fol", gathered, synthesis, preferred_element_type=jnp.float32
    )
    filtered = grid_values.astype(jnp.bfloat16)
    point_rows = field_count * band_rows
    partial_peaks = storm_maxima(
        grid_values.reshape(point_rows, OUT_LON),
        storm_labels.reshape(point_rows, OUT_LON),
        storm_count,
    )
    local_peaks = jnp.max(partial_peaks, axis=(1, 2))
    slot_ids = jnp.arange(storm_count, dtype=jnp.int32)
    by_slot = jnp.max(
        jnp.where(storm_owner[:, None] == slot_ids[None, :], local_peaks[:, None], FLOOR), axis=0
    )
    spec_count = halves * ranks
    shares = lax.all_to_all(
        by_slot.reshape(spec_count, storm_count // spec_count),
        ("half", "rest"),
        split_axis=0,
        concat_axis=0,
        tiled=True,
    )
    return (filtered, jnp.max(shares, axis=0))


def solution(mesh):
    groups = mesh.shape["grp"]
    spec_count = mesh.shape["spec"]
    split = Mesh(
        mesh.devices.reshape(groups, 2, spec_count // 2), axis_names=("grp", "half", "rest")
    )
    both = ("half", "rest")
    return jax.shard_map(
        local,
        mesh=split,
        in_specs=(P("grp", both, None), P(), P("grp", both, None), P("grp")),
        out_specs=(P("grp", both, None), P(("grp", "half", "rest"))),
        check_vma=False,
    )
```

```python
import math

import jax
import jax.numpy as jnp
import numpy as np
from jax import lax
from jax.experimental import pallas as pl
from jax.experimental.pallas import tpu as pltpu
from jax.sharding import Mesh
from jax.sharding import PartitionSpec as P

MW = 256
OUT_LAT = 256
OUT_LON = 720
FLOOR = -1e30
GROUP = 8
LANES = 128
SCAN_ROWS = 4


def fourier_table(lon_count):
    steps = np.arange(lon_count)[:, None] * np.arange(MW)[None, :] % lon_count
    angles = steps * (2.0 * math.pi / lon_count)
    return np.stack([np.cos(angles), -np.sin(angles)], axis=-1) / lon_count


def synthesis_table(lon_count):
    steps = np.arange(MW)[:, None] * np.arange(lon_count)[None, :] % lon_count
    angles = steps * (2.0 * math.pi / lon_count)
    factor = np.where(np.arange(MW) == 0, 1.0, 2.0)[:, None]
    return np.stack([factor * np.cos(angles), -factor * np.sin(angles)], axis=1)


def diagonal_logs():
    counters = np.arange(1, MW, dtype=np.float64)
    increments = np.log((2.0 * counters + 1.0) / (2.0 * counters))
    sums = np.concatenate([[0.0], np.cumsum(increments)])
    return (0.5 * math.log(0.5) + 0.5 * sums).astype(np.float32)


def params(mebibytes):
    return pltpu.CompilerParams(vmem_limit_bytes=mebibytes << 20)


def whole(shape, dtype):
    return jax.ShapeDtypeStruct(shape, dtype)


IN_VMEM = pl.BlockSpec(memory_space=pltpu.VMEM)


def fourier(vorticity, table, senders, parts):
    fields, rows, lon_count = vorticity.shape
    waves = table.shape[1] // 2
    block = 16 if rows % 16 == 0 else 8
    wave_block = waves // parts

    def body(data_ref, table_ref, *refs):
        out_refs, (product_ref, turned_ref) = refs[:parts], refs[parts:]
        data = data_ref[...].reshape(fields * block, lon_count)
        product = jnp.dot(data, table_ref[...], preferred_element_type=jnp.float32)
        for t in range(2 * waves // LANES):
            product_ref[t] = product[:, t * LANES : (t + 1) * LANES]
        for j in range(block):
            for t in range(waves // LANES):
                pair = [
                    product_ref[r * (waves // LANES) + t, pl.ds(j, fields, stride=block), :]
                    for r in range(2)
                ]
                start = t * LANES * block + j
                turned_ref[pl.ds(start, LANES, stride=block), :] = jnp.concatenate(pair, axis=0).T
        for p in range(parts):
            size = wave_block * block
            part = turned_ref[p * size : (p + 1) * size, :]
            out_refs[p][...] = part.astype(jnp.bfloat16).reshape(out_refs[p].shape)

    shape = (senders, wave_block // senders, rows, 2 * fields)
    return pl.pallas_call(
        body,
        out_shape=[whole(shape, jnp.bfloat16)] * parts,
        grid=(rows // block,),
        in_specs=[
            pl.BlockSpec((fields, block, lon_count), lambda i: (0, i, 0)),
            pl.BlockSpec(table.shape, lambda i: (0, 0), pipeline_mode=pl.Buffered(1)),
        ],
        out_specs=[
            pl.BlockSpec((shape[0], shape[1], block, shape[3]), lambda i: (0, 0, i, 0))
        ] * parts,
        scratch_shapes=[
            pltpu.VMEM((2 * waves // LANES, fields * block, LANES), jnp.float32),
            pltpu.VMEM((waves * block, 2 * fields), jnp.float32),
        ],
        compiler_params=params(24),
    )(vorticity, table)


def halves_of(x):
    high = x.astype(jnp.bfloat16)
    return high, (x - high.astype(jnp.float32)).astype(jnp.bfloat16)


def kernel_table(orders, start, cosines, weights, out_rows, offsets):
    columns = start.shape[1]
    in_rows = columns - out_rows
    tiles = columns // LANES
    out_tiles = out_rows // LANES

    def body(order_ref, start_ref, cos_ref, weight_ref, out_ref, table_ref):
        m = jnp.broadcast_to(order_ref[...], (GROUP, LANES))
        cosine = [
            jnp.broadcast_to(cos_ref[:, t * LANES : (t + 1) * LANES], (GROUP, LANES))
            for t in range(tiles)
        ]

        def step(k, carry):
            previous, earlier = carry
            offset = k.astype(jnp.float32)
            degree = m + offset
            below = degree - 1.0
            first = jnp.sqrt((4.0 * degree * degree - 1.0) / (offset * (2.0 * m + offset)))
            second = jnp.sqrt(
                (offset - 1.0)
                * (2.0 * m + offset - 1.0)
                / jnp.maximum(4.0 * below * below - 1.0, 1.0)
            )
            keep = degree <= MW - 1.0
            row = pl.multiple_of(k * GROUP, GROUP)
            current = []
            for t in range(tiles):
                value = first * (cosine[t] * previous[t] - second * earlier[t])
                current.append(value)
                stored = jnp.where(keep, value, 0.0) if t < out_tiles else value
                table_ref[t, pl.ds(row, GROUP), :] = stored
            return (tuple(current), previous)

        first_rows = tuple(start_ref[:, t * LANES : (t + 1) * LANES] for t in range(tiles))
        for t in range(tiles):
            table_ref[t, 0:GROUP, :] = first_rows[t]
        zeros = tuple(jnp.zeros((GROUP, LANES), jnp.float32) for _ in range(tiles))
        first_step = step(jnp.int32(1), (first_rows, zeros))
        second_step = step(jnp.int32(2), first_step)
        third_step = step(jnp.int32(3), second_step)
        lax.fori_loop(4, offsets, step, third_step, unroll=4)
        weight = weight_ref[...]
        for s in range(GROUP):
            values = [table_ref[t, pl.ds(s, offsets, stride=GROUP), :] for t in range(tiles)]
            out_high, out_low = halves_of(jnp.concatenate(values[:out_tiles], axis=1))
            in_high, in_low = halves_of(jnp.concatenate(values[out_tiles:], axis=1))
            product = lax.dot_general(
                jnp.concatenate([out_high, out_high, out_low], axis=0),
                jnp.concatenate([in_high, in_low, in_high], axis=0),
                (((0,), (0,)), ((), ())),
                preferred_element_type=jnp.float32,
            )
            out_ref[s] = (product * weight).astype(jnp.bfloat16)

    return pl.pallas_call(
        body,
        out_shape=whole((GROUP, out_rows, in_rows), jnp.bfloat16),
        in_specs=[IN_VMEM] * 4,
        out_specs=IN_VMEM,
        scratch_shapes=[pltpu.VMEM((tiles, offsets * GROUP, LANES), jnp.float32)],
        compiler_params=params(24),
    )(orders, start, cosines, weights)


def apply_table(table, received):
    senders, slots, rows, columns = received.shape
    out_rows = table.shape[1]
    half = out_rows // 2

    def body(table_ref, data_ref, own_ref, other_ref, wide_ref):
        for s in range(slots):
            data = data_ref[:, s].reshape(senders * rows, columns)
            product = jnp.dot(table_ref[s], data, preferred_element_type=jnp.float32)
            own_ref[pl.ds(s, half, stride=slots), :] = product[:half]
            wide_ref[pl.ds(s, half, stride=slots), :] = product[half:]
        other_ref[...] = wide_ref[...].astype(jnp.bfloat16)

    return pl.pallas_call(
        body,
        out_shape=(
            whole((half * slots, columns), jnp.float32),
            whole((half * slots, columns), jnp.bfloat16),
        ),
        in_specs=[IN_VMEM] * 2,
        out_specs=(IN_VMEM, IN_VMEM),
        scratch_shapes=[pltpu.VMEM((half * slots, columns), jnp.float32)],
        compiler_params=params(16),
    )(table, received)


def storm_maxima(values, labels, storm_count):
    rows, lon_count = values.shape
    block = math.gcd(rows, 512)
    steps = rows // block
    tiles = -(-lon_count // LANES)
    tail = lon_count - (tiles - 1) * LANES
    span = math.gcd(block, 256)
    sets = [(t, r) for t in range(tiles) for r in range(0, block, span)]
    chosen = steps * len(sets)

    def body(value_ref, label_ref, out_ref, kept_ref, name_ref, best_ref, storm_ref, top_ref):
        step = pl.program_id(0)

        @pl.when(step == 0)
        def _():
            kept_ref[tiles - 1] = jnp.full((rows, LANES), FLOOR, jnp.float32)
            name_ref[tiles - 1] = jnp.full((rows, LANES), storm_count, jnp.int32)

        base = pl.multiple_of(step * block, block)
        for t in range(tiles):
            width = LANES if t < tiles - 1 else tail
            columns = slice(t * LANES, t * LANES + width)
            name = label_ref[:, columns]
            value = jnp.where(name < storm_count, value_ref[:, columns], FLOOR)
            kept_ref[t, pl.ds(base, block), 0:width] = value
            name_ref[t, pl.ds(base, block), 0:width] = name
        for s, (t, r) in enumerate(sets):
            best = jnp.full((8, LANES), FLOOR, jnp.float32)
            storm = jnp.zeros((8, LANES), jnp.int32)
            for i in range(r, r + span, 8):
                value = kept_ref[t, pl.ds(base + i, 8), :]
                name = name_ref[t, pl.ds(base + i, 8), :]
                higher = value > best
                best = jnp.where(higher, value, best)
                storm = jnp.where(higher, name, storm)
            best_ref[step * len(sets) + s] = best
            storm_ref[step * len(sets) + s] = storm

        def raise_tops(bests, storms):
            def per_storm(i, carry):
                picked = [jnp.where(storm == i, best, FLOOR) for best, storm in zip(bests, storms)]
                while len(picked) > 1:
                    paired = [jnp.maximum(a, b) for a, b in zip(picked[::2], picked[1::2])]
                    picked = paired + picked[2 * len(paired):]
                top = jnp.max(picked[0], axis=0, keepdims=True)
                top_ref[pl.ds(i, 1), :] = jnp.maximum(top_ref[pl.ds(i, 1), :], top)
                return carry

            lax.fori_loop(0, storm_count, per_storm, 0, unroll=8)

        def merge(a, b):
            higher = b[0] > a[0]
            return (jnp.where(higher, b[0], a[0]), jnp.where(higher, b[1], a[1]), a[2] + b[2])

        def tops():
            return jnp.max(top_ref[...].T, axis=0, keepdims=True)

        @pl.when(step == steps - 1)
        def _():
            top_ref[...] = jnp.full(top_ref.shape, FLOOR, jnp.float32)
            raise_tops([best_ref[c] for c in range(chosen)], [storm_ref[c] for c in range(chosen)])

            def scan(carry):
                top = tops()
                table = [
                    jnp.broadcast_to(top[:, h * LANES : (h + 1) * LANES], (8, LANES))
                    for h in range(storm_count // LANES)
                ]
                tiny = jnp.zeros((8, LANES), jnp.float32)

                def per_rows(i, state):
                    row = pl.multiple_of(i * (8 * SCAN_ROWS), 8 * SCAN_ROWS)
                    found = []
                    for r in range(SCAN_ROWS):
                        for t in range(tiles):
                            value = kept_ref[t, pl.ds(row + 8 * r, 8), :]
                            name = name_ref[t, pl.ds(row + 8 * r, 8), :]
                            place = jnp.bitwise_and(name, LANES - 1)
                            known = jnp.take_along_axis(table[0], place, axis=1)
                            for h in range(1, len(table)):
                                other = jnp.take_along_axis(table[h], place, axis=1)
                                known = jnp.where(name >= h * LANES, other, known)
                            open_ = value > known
                            found.append(
                                (jnp.where(open_, value, FLOOR), name, jnp.where(open_, 1.0, 0.0))
                            )
                    while len(found) > 1:
                        paired = [merge(a, b) for a, b in zip(found[::2], found[1::2])]
                        found = paired + found[2 * len(paired):]
                    return merge(state, found[0])

                init = (jnp.full((8, LANES), FLOOR, jnp.float32), jnp.zeros((8, LANES), jnp.int32), tiny)
                best, storm, count = lax.fori_loop(0, rows // (8 * SCAN_ROWS), per_rows, init)
                most = jnp.max(count)

                @pl.when(most > 0.0)
                def _():
                    raise_tops([best], [storm])

                return most

            lax.while_loop(lambda most: most > 1.0, scan, jnp.float32(2.0))
            out_ref[...] = tops()

    return pl.pallas_call(
        body,
        out_shape=jax.ShapeDtypeStruct((1, storm_count), jnp.float32),
        grid=(steps,),
        in_specs=[
            pl.BlockSpec((block, lon_count), lambda i: (i, 0)),
            pl.BlockSpec((block, lon_count), lambda i: (i, 0)),
        ],
        out_specs=pl.BlockSpec((1, storm_count), lambda i: (0, 0)),
        scratch_shapes=[
            pltpu.VMEM((tiles, rows, LANES), jnp.float32),
            pltpu.VMEM((tiles, rows, LANES), jnp.int32),
            pltpu.VMEM((chosen, 8, LANES), jnp.float32),
            pltpu.VMEM((chosen, 8, LANES), jnp.int32),
            pltpu.VMEM((storm_count, LANES), jnp.float32),
        ],
        compiler_params=params(32),
    )(values, labels)

def local(vorticity, lat_order, storm_labels, storm_owner):
    field_count, lat_rows, lon_count = vorticity.shape
    lat_count = lat_order.shape[0]
    halves = lax.axis_size("half")
    ranks = lax.axis_size("rest")
    half_index = lax.axis_index("half")
    rank = lax.axis_index("rest")
    band_rows = storm_labels.shape[1]
    storm_count = storm_owner.shape[0]
    slots = MW // ranks
    chunks = slots // GROUP
    columns = 2 * field_count
    out_half = OUT_LAT // halves

    parts = min(2, chunks)
    calls = chunks // parts
    table = fourier_table(lon_count).reshape(lon_count, calls, parts, GROUP, ranks, 2)
    table = table.transpose(1, 0, 5, 2, 4, 3).reshape(calls, lon_count, 2 * MW // calls)
    table = table.astype(jnp.bfloat16)

    received = []
    for c in range(calls):
        for coefficients in fourier(vorticity, jnp.asarray(table[c]), ranks, parts):
            received.append(
                lax.all_to_all(coefficients, "rest", split_axis=0, concat_axis=0, tiled=True)
            )

    half_rows = ranks * lat_rows
    own_order = lax.dynamic_slice_in_dim(lat_order, half_index * half_rows, half_rows)
    colatitude = math.pi * (4.0 * own_order.astype(jnp.float32) + 3.0) / (4.0 * lat_count + 2.0)
    weights = math.pi / lat_count * jnp.sin(colatitude)
    band_index = jnp.arange(OUT_LAT, dtype=jnp.int32)
    band_index = ((band_index + half_index * out_half) % OUT_LAT).astype(jnp.float32)
    latitude = ((OUT_LAT - 1) / 2.0 - band_index) * (360.0 / OUT_LON) * (math.pi / 180.0)
    sine_values = jnp.concatenate([jnp.cos(latitude), jnp.sin(colatitude)])
    cosines = jnp.concatenate([jnp.sin(latitude), jnp.cos(colatitude)])
    orders = jnp.arange(slots, dtype=jnp.int32) * ranks + rank
    start_logs = jnp.asarray(diagonal_logs().reshape(slots, ranks))
    start_logs = lax.dynamic_slice_in_dim(start_logs, rank, 1, axis=1)
    orders = orders.astype(jnp.float32)[:, None]
    start = jnp.exp(start_logs + orders * jnp.log(sine_values)[None, :])
    kernels = [
        kernel_table(
            orders[c * GROUP : (c + 1) * GROUP],
            start[c * GROUP : (c + 1) * GROUP],
            cosines[None, :],
            weights[None, :],
            OUT_LAT,
            MW - c * GROUP * ranks,
        )
        for c in range(chunks)
    ]

    partial = [apply_table(kernels[c], received[c]) for c in range(chunks)]
    gathered = []
    swap = [(0, 1), (1, 0)]
    for own, other in partial:
        mirrored = lax.ppermute(other, "half", swap)
        band = (own + mirrored.astype(jnp.float32)).astype(jnp.bfloat16)
        band = band.reshape(ranks, band_rows * GROUP, columns)
        band = lax.all_to_all(band, "rest", split_axis=0, concat_axis=0, tiled=True)
        gathered.append(band.reshape(ranks, band_rows, GROUP, 2, field_count))

    gathered = jnp.stack(gathered)
    synthesis = synthesis_table(OUT_LON).reshape(chunks, GROUP, ranks, 2, OUT_LON)
    synthesis = jnp.asarray(synthesis.transpose(0, 2, 1, 3, 4).astype(jnp.bfloat16))
    grid_values = jnp.einsum(
        "cqosrf,cqsrl->fol", gathered, synthesis, preferred_element_type=jnp.float32
    )
    filtered = grid_values.astype(jnp.bfloat16)
    point_rows = field_count * band_rows
    local_peaks = storm_maxima(
        grid_values.reshape(point_rows, OUT_LON),
        storm_labels.reshape(point_rows, OUT_LON),
        storm_count,
    )[0]
    slot_ids = jnp.arange(storm_count, dtype=jnp.int32)
    by_slot = jnp.max(
        jnp.where(storm_owner[:, None] == slot_ids[None, :], local_peaks[:, None], FLOOR), axis=0
    )
    spec_count = halves * ranks
    shares = lax.all_to_all(
        by_slot.reshape(spec_count, storm_count // spec_count),
        ("half", "rest"),
        split_axis=0,
        concat_axis=0,
        tiled=True,
    )
    return (filtered, jnp.max(shares, axis=0))


def solution(mesh):
    groups = mesh.shape["grp"]
    spec_count = mesh.shape["spec"]
    split = Mesh(
        mesh.devices.reshape(groups, 2, spec_count // 2), axis_names=("grp", "half", "rest")
    )
    both = ("half", "rest")
    return jax.shard_map(
        local,
        mesh=split,
        in_specs=(P("grp", both, None), P(), P("grp", both, None), P("grp")),
        out_specs=(P("grp", both, None), P(("grp", "half", "rest"))),
        check_vma=False,
    )
```

```python
import functools
import math

import jax
import jax.numpy as jnp
import numpy as np
from jax import lax
from jax.experimental import pallas as pl
from jax.experimental.pallas import tpu as pltpu
from jax.sharding import Mesh
from jax.sharding import PartitionSpec as P

MW = 256
OUT_LAT = 256
OUT_LON = 720
FLOOR = -1e30
GROUP = 8
LANES = 128
SCAN_ROWS = 4


def fourier_table(lon_count):
    steps = np.arange(lon_count)[:, None] * np.arange(MW)[None, :] % lon_count
    angles = steps * (2.0 * math.pi / lon_count)
    return np.stack([np.cos(angles), -np.sin(angles)], axis=-1) / lon_count


def synthesis_table(lon_count):
    steps = np.arange(MW)[:, None] * np.arange(lon_count)[None, :] % lon_count
    angles = steps * (2.0 * math.pi / lon_count)
    factor = np.where(np.arange(MW) == 0, 1.0, 2.0)[:, None]
    return np.stack([factor * np.cos(angles), -factor * np.sin(angles)], axis=1)


def diagonal_logs():
    counters = np.arange(1, MW, dtype=np.float64)
    increments = np.log((2.0 * counters + 1.0) / (2.0 * counters))
    sums = np.concatenate([[0.0], np.cumsum(increments)])
    return (0.5 * math.log(0.5) + 0.5 * sums).astype(np.float32)


def params(mebibytes):
    return pltpu.CompilerParams(vmem_limit_bytes=mebibytes << 20)


def whole(shape, dtype):
    return jax.ShapeDtypeStruct(shape, dtype)


IN_VMEM = pl.BlockSpec(memory_space=pltpu.VMEM)


def fourier(vorticity, table, senders, part_slots):
    fields, rows, lon_count = vorticity.shape
    waves = table.shape[1] // 2
    block = 16 if rows % 16 == 0 else 8
    parts = len(part_slots)

    def body(data_ref, table_ref, *refs):
        out_refs, (product_ref, turned_ref) = refs[:parts], refs[parts:]
        data = data_ref[...].reshape(fields * block, lon_count)
        product = jnp.dot(data, table_ref[...], preferred_element_type=jnp.float32)
        for t in range(2 * waves // LANES):
            product_ref[t] = product[:, t * LANES : (t + 1) * LANES]
        for j in range(block):
            for t in range(waves // LANES):
                pair = [
                    product_ref[r * (waves // LANES) + t, pl.ds(j, fields, stride=block), :]
                    for r in range(2)
                ]
                start = t * LANES * block + j
                turned_ref[pl.ds(start, LANES, stride=block), :] = jnp.concatenate(pair, axis=0).T
        start = 0
        for p in range(parts):
            size = senders * part_slots[p] * block
            part = turned_ref[start : start + size, :]
            out_refs[p][...] = part.astype(jnp.bfloat16).reshape(out_refs[p].shape)
            start += size

    return pl.pallas_call(
        body,
        out_shape=[whole((senders, n, rows, 2 * fields), jnp.bfloat16) for n in part_slots],
        grid=(rows // block,),
        in_specs=[
            pl.BlockSpec((fields, block, lon_count), lambda i: (0, i, 0)),
            pl.BlockSpec(table.shape, lambda i: (0, 0), pipeline_mode=pl.Buffered(1)),
        ],
        out_specs=[
            pl.BlockSpec((senders, n, block, 2 * fields), lambda i: (0, 0, i, 0)) for n in part_slots
        ],
        scratch_shapes=[
            pltpu.VMEM((2 * waves // LANES, fields * block, LANES), jnp.float32),
            pltpu.VMEM((waves * block, 2 * fields), jnp.float32),
        ],
        compiler_params=params(24),
    )(pltpu.with_memory_space_constraint(vorticity, pltpu.HBM), table)


def halves_of(x):
    high = x.astype(jnp.bfloat16)
    return high, (x - high.astype(jnp.float32)).astype(jnp.bfloat16)


def kernel_table(orders, start, cosines, weights, out_rows, offsets):
    columns = start.shape[1]
    in_rows = columns - out_rows
    tiles = columns // LANES
    out_tiles = out_rows // LANES

    def body(order_ref, start_ref, cos_ref, weight_ref, out_ref, table_ref):
        m = jnp.broadcast_to(order_ref[...], (GROUP, LANES))
        cosine = [
            jnp.broadcast_to(cos_ref[:, t * LANES : (t + 1) * LANES], (GROUP, LANES))
            for t in range(tiles)
        ]

        def step(k, carry):
            previous, earlier = carry
            offset = k.astype(jnp.float32)
            degree = m + offset
            below = degree - 1.0
            first = jnp.sqrt((4.0 * degree * degree - 1.0) / (offset * (2.0 * m + offset)))
            second = jnp.sqrt(
                (offset - 1.0)
                * (2.0 * m + offset - 1.0)
                / jnp.maximum(4.0 * below * below - 1.0, 1.0)
            )
            keep = degree <= MW - 1.0
            row = pl.multiple_of(k * GROUP, GROUP)
            current = []
            for t in range(tiles):
                value = first * (cosine[t] * previous[t] - second * earlier[t])
                current.append(value)
                stored = jnp.where(keep, value, 0.0) if t < out_tiles else value
                table_ref[t, pl.ds(row, GROUP), :] = stored
            return (tuple(current), previous)

        first_rows = tuple(start_ref[:, t * LANES : (t + 1) * LANES] for t in range(tiles))
        for t in range(tiles):
            table_ref[t, 0:GROUP, :] = first_rows[t]
        zeros = tuple(jnp.zeros((GROUP, LANES), jnp.float32) for _ in range(tiles))
        first_step = step(jnp.int32(1), (first_rows, zeros))
        second_step = step(jnp.int32(2), first_step)
        third_step = step(jnp.int32(3), second_step)
        lax.fori_loop(4, offsets, step, third_step, unroll=4)
        weight = weight_ref[...]
        for s in range(GROUP):
            values = [table_ref[t, pl.ds(s, offsets, stride=GROUP), :] for t in range(tiles)]
            out_high, out_low = halves_of(jnp.concatenate(values[:out_tiles], axis=1))
            in_high, in_low = halves_of(jnp.concatenate(values[out_tiles:], axis=1))
            product = lax.dot_general(
                jnp.concatenate([out_high, out_high, out_low], axis=0),
                jnp.concatenate([in_high, in_low, in_high], axis=0),
                (((0,), (0,)), ((), ())),
                preferred_element_type=jnp.float32,
            )
            out_ref[s] = (product * weight).astype(jnp.bfloat16)

    return pl.pallas_call(
        body,
        out_shape=whole((GROUP, out_rows, in_rows), jnp.bfloat16),
        in_specs=[IN_VMEM] * 4,
        out_specs=IN_VMEM,
        scratch_shapes=[pltpu.VMEM((tiles, offsets * GROUP, LANES), jnp.float32)],
        compiler_params=params(24),
    )(orders, start, cosines, weights)


def apply_tables(tables, received):
    senders, slots, rows, columns = received.shape
    out_rows = tables[0].shape[1]
    half = out_rows // 2

    def body(*refs):
        table_refs, (data_ref, own_ref, other_ref, wide_ref) = refs[: len(tables)], refs[len(tables) :]
        for s in range(slots):
            data = data_ref[:, s].reshape(senders * rows, columns)
            table = table_refs[s // GROUP][s % GROUP]
            product = jnp.dot(table, data, preferred_element_type=jnp.float32)
            own_ref[pl.ds(s, half, stride=slots), :] = product[:half]
            wide_ref[pl.ds(s, half, stride=slots), :] = product[half:]
        other_ref[...] = wide_ref[...].astype(jnp.bfloat16)

    return pl.pallas_call(
        body,
        out_shape=(
            whole((half * slots, columns), jnp.float32),
            whole((half * slots, columns), jnp.bfloat16),
        ),
        in_specs=[IN_VMEM] * (len(tables) + 1),
        out_specs=(IN_VMEM, IN_VMEM),
        scratch_shapes=[pltpu.VMEM((half * slots, columns), jnp.float32)],
        compiler_params=params(16),
    )(*tables, received)


def storm_maxima(values, labels, storm_count):
    rows, lon_count = values.shape
    block = math.gcd(rows, 512)
    steps = rows // block
    tiles = -(-lon_count // LANES)
    tail = lon_count - (tiles - 1) * LANES
    span = math.gcd(block, 256)
    sets = [(t, r) for t in range(tiles) for r in range(0, block, span)]
    chosen = steps * len(sets)

    def body(value_ref, label_ref, out_ref, kept_ref, name_ref, best_ref, storm_ref, top_ref):
        step = pl.program_id(0)

        @pl.when(step == 0)
        def _():
            kept_ref[tiles - 1] = jnp.full((rows, LANES), FLOOR, jnp.float32)
            name_ref[tiles - 1] = jnp.full((rows, LANES), storm_count, jnp.int32)

        base = pl.multiple_of(step * block, block)
        for t in range(tiles):
            width = LANES if t < tiles - 1 else tail
            columns = slice(t * LANES, t * LANES + width)
            name = label_ref[:, columns]
            value = jnp.where(name < storm_count, value_ref[:, columns], FLOOR)
            kept_ref[t, pl.ds(base, block), 0:width] = value
            name_ref[t, pl.ds(base, block), 0:width] = name
        for s, (t, r) in enumerate(sets):
            best = jnp.full((8, LANES), FLOOR, jnp.float32)
            storm = jnp.zeros((8, LANES), jnp.int32)
            for i in range(r, r + span, 8):
                value = kept_ref[t, pl.ds(base + i, 8), :]
                name = name_ref[t, pl.ds(base + i, 8), :]
                higher = value > best
                best = jnp.where(higher, value, best)
                storm = jnp.where(higher, name, storm)
            best_ref[step * len(sets) + s] = best
            storm_ref[step * len(sets) + s] = storm

        def raise_tops(bests, storms):
            def per_storm(i, carry):
                picked = [jnp.where(storm == i, best, FLOOR) for best, storm in zip(bests, storms)]
                while len(picked) > 1:
                    paired = [jnp.maximum(a, b) for a, b in zip(picked[::2], picked[1::2])]
                    picked = paired + picked[2 * len(paired):]
                top = jnp.max(picked[0], axis=0, keepdims=True)
                top_ref[pl.ds(i, 1), :] = jnp.maximum(top_ref[pl.ds(i, 1), :], top)
                return carry

            lax.fori_loop(0, storm_count, per_storm, 0, unroll=8)

        def merge(a, b):
            higher = b[0] > a[0]
            return (jnp.where(higher, b[0], a[0]), jnp.where(higher, b[1], a[1]), a[2] + b[2])

        def tops():
            return jnp.max(top_ref[...].T, axis=0, keepdims=True)

        @pl.when(step == steps - 1)
        def _():
            top_ref[...] = jnp.full(top_ref.shape, FLOOR, jnp.float32)
            raise_tops([best_ref[c] for c in range(chosen)], [storm_ref[c] for c in range(chosen)])

            def scan(carry):
                top = tops()
                table = [
                    jnp.broadcast_to(top[:, h * LANES : (h + 1) * LANES], (8, LANES))
                    for h in range(storm_count // LANES)
                ]
                tiny = jnp.zeros((8, LANES), jnp.float32)

                def per_rows(i, state):
                    row = pl.multiple_of(i * (8 * SCAN_ROWS), 8 * SCAN_ROWS)
                    merged = []
                    for t in range(tiles):
                        found = [state[t]]
                        for r in range(SCAN_ROWS):
                            value = kept_ref[t, pl.ds(row + 8 * r, 8), :]
                            name = name_ref[t, pl.ds(row + 8 * r, 8), :]
                            place = jnp.bitwise_and(name, LANES - 1)
                            known = jnp.take_along_axis(table[0], place, axis=1)
                            for h in range(1, len(table)):
                                other = jnp.take_along_axis(table[h], place, axis=1)
                                known = jnp.where(name >= h * LANES, other, known)
                            is_open = value > known
                            found.append(
                                (
                                    jnp.where(is_open, value, FLOOR),
                                    name,
                                    jnp.where(is_open, 1.0, 0.0),
                                )
                            )
                        while len(found) > 1:
                            paired = [merge(a, b) for a, b in zip(found[::2], found[1::2])]
                            found = paired + found[2 * len(paired) :]
                        merged.append(found[0])
                    return tuple(merged)

                floor = jnp.full((8, LANES), FLOOR, jnp.float32)
                init = ((floor, jnp.zeros((8, LANES), jnp.int32), tiny),) * tiles
                state = lax.fori_loop(0, rows // (8 * SCAN_ROWS), per_rows, init)
                count = functools.reduce(jnp.maximum, [part[2] for part in state])
                most = jnp.max(count)

                @pl.when(most > 0.0)
                def _():
                    raise_tops([part[0] for part in state], [part[1] for part in state])

                return most

            lax.while_loop(lambda most: most > 1.0, scan, jnp.float32(2.0))
            out_ref[...] = tops()

    return pl.pallas_call(
        body,
        out_shape=jax.ShapeDtypeStruct((1, storm_count), jnp.float32),
        grid=(steps,),
        in_specs=[
            pl.BlockSpec((block, lon_count), lambda i: (i, 0)),
            pl.BlockSpec((block, lon_count), lambda i: (i, 0)),
        ],
        out_specs=pl.BlockSpec((1, storm_count), lambda i: (0, 0)),
        scratch_shapes=[
            pltpu.VMEM((tiles, rows, LANES), jnp.float32),
            pltpu.VMEM((tiles, rows, LANES), jnp.int32),
            pltpu.VMEM((chosen, 8, LANES), jnp.float32),
            pltpu.VMEM((chosen, 8, LANES), jnp.int32),
            pltpu.VMEM((storm_count, LANES), jnp.float32),
        ],
        compiler_params=params(32),
    )(values, labels)

def after(x, *others):
    return lax.optimization_barrier((x, *others))[0]


def local(vorticity, lat_order, storm_labels, storm_owner):
    field_count, lat_rows, lon_count = vorticity.shape
    lat_count = lat_order.shape[0]
    halves = lax.axis_size("half")
    ranks = lax.axis_size("rest")
    half_index = lax.axis_index("half")
    rank = lax.axis_index("rest")
    band_rows = storm_labels.shape[1]
    storm_count = storm_owner.shape[0]
    slots = MW // ranks
    chunks = slots // GROUP
    columns = 2 * field_count
    out_half = OUT_LAT // halves

    calls = [[16], [8, 8]] if slots == 32 else [[slots // 2], [slots // 2]]
    full_table = fourier_table(lon_count).reshape(lon_count, slots, ranks, 2)
    coefficients = []
    first = 0
    for part_slots in calls:
        pieces = []
        base = first
        for n in part_slots:
            pieces.append(full_table[:, base : base + n].transpose(0, 2, 1, 3).reshape(lon_count, -1, 2))
            base += n
        table = np.concatenate(pieces, axis=1).transpose(0, 2, 1).reshape(lon_count, -1)
        table = jnp.asarray(table.astype(jnp.bfloat16))
        coefficients += fourier(vorticity, table, ranks, part_slots)
        first = base
    stages = [n for part_slots in calls for n in part_slots]
    half_rows = ranks * lat_rows
    own_order = lax.dynamic_slice_in_dim(lat_order, half_index * half_rows, half_rows)
    colatitude = math.pi * (4.0 * own_order.astype(jnp.float32) + 3.0) / (4.0 * lat_count + 2.0)
    weights = math.pi / lat_count * jnp.sin(colatitude)
    band_index = jnp.arange(OUT_LAT, dtype=jnp.int32)
    band_index = ((band_index + half_index * out_half) % OUT_LAT).astype(jnp.float32)
    latitude = ((OUT_LAT - 1) / 2.0 - band_index) * (360.0 / OUT_LON) * (math.pi / 180.0)
    sine_values = jnp.concatenate([jnp.cos(latitude), jnp.sin(colatitude)])
    cosines = jnp.concatenate([jnp.sin(latitude), jnp.cos(colatitude)])
    orders = jnp.arange(slots, dtype=jnp.int32) * ranks + rank
    start_logs = jnp.asarray(diagonal_logs().reshape(slots, ranks))
    start_logs = lax.dynamic_slice_in_dim(start_logs, rank, 1, axis=1)
    orders = orders.astype(jnp.float32)[:, None]
    start = jnp.exp(start_logs + orders * jnp.log(sine_values)[None, :])
    def kernels(begin, end, token):
        ordered = after(start, token)
        return [
            kernel_table(
                orders[c * GROUP : (c + 1) * GROUP],
                ordered[c * GROUP : (c + 1) * GROUP],
                cosines[None, :],
                weights[None, :],
                OUT_LAT,
                MW - c * GROUP * ranks,
            )
            for c in range(begin, end)
        ]

    def exchange(block):
        return lax.all_to_all(block, "rest", split_axis=0, concat_axis=0, tiled=True)

    def swapped(block):
        return lax.ppermute(block, "half", [(0, 1), (1, 0)])

    last_stage = len(stages) - 1
    received = exchange(coefficients[0])
    first = stages[0] // GROUP
    tables = kernels(0, first, coefficients[-1][0, 0, 0, :1])
    done_work = tuple(tables) + tuple(coefficients[1:])
    bands = []
    for i, n in enumerate(stages):
        received = after(received, *done_work)
        following = None
        if i == 1 and i < last_stage:
            received = after(received, early_swap)
        if i < last_stage:
            following = exchange(after(coefficients[i + 1], received))
        own, other = apply_tables(tables, received)
        cut = other.shape[0] // 2
        if i == 0:
            early_swap = swapped(other[:cut])
            mirrored = jnp.concatenate([early_swap, swapped(other[cut:])])
            later = kernels(first, slots // GROUP, other[0, :1])
            done_work = (other, *later)
        else:
            mirrored = swapped(other)
            done_work = (other, *bands)
        taken = sum(stages[: i + 1]) // GROUP - first
        if i < last_stage:
            tables = later[taken : taken + stages[i + 1] // GROUP]
        band = (own + mirrored.astype(jnp.float32)).astype(jnp.bfloat16)
        bands.append(band.reshape(ranks, band_rows * n, columns))
        last_received, received = received, following

    early = jnp.concatenate(bands[:-1], axis=1)
    early = exchange(after(early, last_received))
    late = exchange(after(bands[-1], early))
    early = early.reshape(ranks, -1, columns)
    late = late.reshape(ranks, -1, columns)
    gathered = []
    first = 0
    for i, n in enumerate(stages):
        block = late
        if i < last_stage:
            block = early[:, first : first + band_rows * n]
            first += band_rows * n
        gathered.append(block.reshape(ranks, band_rows, n, 2, field_count))

    gathered = jnp.concatenate(gathered, axis=2)
    synthesis = synthesis_table(OUT_LON).reshape(slots, ranks, 2, OUT_LON)
    synthesis = jnp.asarray(synthesis.transpose(1, 0, 2, 3).astype(jnp.bfloat16))
    grid_values = jnp.einsum(
        "qosrf,qsrl->fol", gathered, synthesis, preferred_element_type=jnp.float32
    )
    filtered = grid_values.astype(jnp.bfloat16)
    point_rows = field_count * band_rows
    local_peaks = storm_maxima(
        grid_values.reshape(point_rows, OUT_LON),
        storm_labels.reshape(point_rows, OUT_LON),
        storm_count,
    )[0]
    slot_ids = jnp.arange(storm_count, dtype=jnp.int32)
    by_slot = jnp.max(
        jnp.where(storm_owner[:, None] == slot_ids[None, :], local_peaks[:, None], FLOOR), axis=0
    )
    spec_count = halves * ranks
    shares = lax.all_to_all(
        by_slot.reshape(spec_count, storm_count // spec_count),
        ("half", "rest"),
        split_axis=0,
        concat_axis=0,
        tiled=True,
    )
    return (filtered, jnp.max(shares, axis=0))


def solution(mesh):
    groups = mesh.shape["grp"]
    spec_count = mesh.shape["spec"]
    split = Mesh(
        mesh.devices.reshape(groups, 2, spec_count // 2), axis_names=("grp", "half", "rest")
    )
    both = ("half", "rest")
    return jax.shard_map(
        local,
        mesh=split,
        in_specs=(P("grp", both, None), P(), P("grp", both, None), P("grp")),
        out_specs=(P("grp", both, None), P(("grp", "half", "rest"))),
        check_vma=False,
    )
```

```python
import functools
import math

import jax
import jax.numpy as jnp
import numpy as np
from jax import lax
from jax.experimental import pallas as pl
from jax.experimental.pallas import tpu as pltpu
from jax.sharding import Mesh
from jax.sharding import PartitionSpec as P

MW = 256
OUT_LAT = 256
OUT_LON = 720
FLOOR = -1e30
GROUP = 8
LANES = 128
SCAN_ROWS = 4


def fourier_table(lon_count):
    steps = np.arange(lon_count)[:, None] * np.arange(MW)[None, :] % lon_count
    angles = steps * (2.0 * math.pi / lon_count)
    return np.stack([np.cos(angles), -np.sin(angles)], axis=-1) / lon_count


def synthesis_table(lon_count):
    steps = np.arange(MW)[:, None] * np.arange(lon_count)[None, :] % lon_count
    angles = steps * (2.0 * math.pi / lon_count)
    factor = np.where(np.arange(MW) == 0, 1.0, 2.0)[:, None]
    return np.stack([factor * np.cos(angles), -factor * np.sin(angles)], axis=1)


def diagonal_logs():
    counters = np.arange(1, MW, dtype=np.float64)
    increments = np.log((2.0 * counters + 1.0) / (2.0 * counters))
    sums = np.concatenate([[0.0], np.cumsum(increments)])
    return (0.5 * math.log(0.5) + 0.5 * sums).astype(np.float32)


def params(mebibytes):
    return pltpu.CompilerParams(vmem_limit_bytes=mebibytes << 20)


def whole(shape, dtype):
    return jax.ShapeDtypeStruct(shape, dtype)


IN_VMEM = pl.BlockSpec(memory_space=pltpu.VMEM)


def fourier(vorticity, table, senders, part_slots):
    fields, rows, lon_count = vorticity.shape
    waves = table.shape[1] // 2
    block = 16 if rows % 16 == 0 else 8
    parts = len(part_slots)

    def body(data_ref, table_ref, *refs):
        out_refs, (product_ref, turned_ref) = refs[:parts], refs[parts:]
        data = data_ref[...].reshape(fields * block, lon_count)
        product = jnp.dot(data, table_ref[...], preferred_element_type=jnp.float32)
        for t in range(2 * waves // LANES):
            product_ref[t] = product[:, t * LANES : (t + 1) * LANES]
        for j in range(block):
            for t in range(waves // LANES):
                pair = [
                    product_ref[r * (waves // LANES) + t, pl.ds(j, fields, stride=block), :]
                    for r in range(2)
                ]
                start = t * LANES * block + j
                turned_ref[pl.ds(start, LANES, stride=block), :] = jnp.concatenate(pair, axis=0).T
        start = 0
        for p in range(parts):
            size = senders * part_slots[p] * block
            part = turned_ref[start : start + size, :]
            out_refs[p][...] = part.astype(jnp.bfloat16).reshape(out_refs[p].shape)
            start += size

    return pl.pallas_call(
        body,
        out_shape=[whole((senders, n, rows, 2 * fields), jnp.bfloat16) for n in part_slots],
        grid=(rows // block,),
        in_specs=[
            pl.BlockSpec((fields, block, lon_count), lambda i: (0, i, 0)),
            pl.BlockSpec(table.shape, lambda i: (0, 0), pipeline_mode=pl.Buffered(1)),
        ],
        out_specs=[
            pl.BlockSpec((senders, n, block, 2 * fields), lambda i: (0, 0, i, 0)) for n in part_slots
        ],
        scratch_shapes=[
            pltpu.VMEM((2 * waves // LANES, fields * block, LANES), jnp.float32),
            pltpu.VMEM((waves * block, 2 * fields), jnp.float32),
        ],
        compiler_params=params(20),
    )(pltpu.with_memory_space_constraint(vorticity, pltpu.HBM), table)


def halves_of(x):
    high = x.astype(jnp.bfloat16)
    return high, (x - high.astype(jnp.float32)).astype(jnp.bfloat16)


def kernel_table(orders, start, cosines, weights, out_rows, offsets, split_rows):
    columns = start.shape[1]
    in_rows = columns - out_rows
    tiles = columns // LANES
    out_tiles = out_rows // LANES

    def body(order_ref, start_ref, cos_ref, weight_ref, *refs):
        out_refs, table_ref = refs[:-1], refs[-1]
        m = jnp.broadcast_to(order_ref[...], (GROUP, LANES))
        cosine = [
            jnp.broadcast_to(cos_ref[:, t * LANES : (t + 1) * LANES], (GROUP, LANES))
            for t in range(tiles)
        ]

        def step(k, carry):
            previous, earlier = carry
            offset = k.astype(jnp.float32)
            degree = m + offset
            below = degree - 1.0
            first = jnp.sqrt((4.0 * degree * degree - 1.0) / (offset * (2.0 * m + offset)))
            second = jnp.sqrt(
                (offset - 1.0)
                * (2.0 * m + offset - 1.0)
                / jnp.maximum(4.0 * below * below - 1.0, 1.0)
            )
            keep = degree <= MW - 1.0
            row = pl.multiple_of(k * GROUP, GROUP)
            current = []
            for t in range(tiles):
                value = first * (cosine[t] * previous[t] - second * earlier[t])
                current.append(value)
                stored = jnp.where(keep, value, 0.0) if t < out_tiles else value
                table_ref[t, pl.ds(row, GROUP), :] = stored
            return (tuple(current), previous)

        first_rows = tuple(start_ref[:, t * LANES : (t + 1) * LANES] for t in range(tiles))
        for t in range(tiles):
            table_ref[t, 0:GROUP, :] = first_rows[t]
        zeros = tuple(jnp.zeros((GROUP, LANES), jnp.float32) for _ in range(tiles))
        first_step = step(jnp.int32(1), (first_rows, zeros))
        second_step = step(jnp.int32(2), first_step)
        third_step = step(jnp.int32(3), second_step)
        lax.fori_loop(4, offsets, step, third_step, unroll=4)
        weight = weight_ref[...]
        for s in range(GROUP):
            values = [table_ref[t, pl.ds(s, offsets, stride=GROUP), :] for t in range(tiles)]
            if split_rows:
                inward = jnp.concatenate(values[out_tiles:], axis=1) * weight
                out_refs[0][s] = inward.astype(jnp.bfloat16)
                outward = jnp.concatenate(values[: split_rows // LANES], axis=1)
                out_refs[1][s] = outward.T.astype(jnp.bfloat16)
                continue
            out_high, out_low = halves_of(jnp.concatenate(values[:out_tiles], axis=1))
            in_high, in_low = halves_of(jnp.concatenate(values[out_tiles:], axis=1))
            product = lax.dot_general(
                jnp.concatenate([out_high, out_high, out_low], axis=0),
                jnp.concatenate([in_high, in_low, in_high], axis=0),
                (((0,), (0,)), ((), ())),
                preferred_element_type=jnp.float32,
            )
            out_refs[0][s] = (product * weight).astype(jnp.bfloat16)

    out_shape = [whole((GROUP, out_rows, in_rows), jnp.bfloat16)]
    if split_rows:
        out_shape = [
            whole((GROUP, offsets, in_rows), jnp.bfloat16),
            whole((GROUP, split_rows, offsets), jnp.bfloat16),
        ]
    return pl.pallas_call(
        body,
        out_shape=out_shape,
        in_specs=[IN_VMEM] * 4,
        out_specs=[IN_VMEM] * len(out_shape),
        scratch_shapes=[pltpu.VMEM((tiles, offsets * GROUP, LANES), jnp.float32)],
        compiler_params=params(14),
    )(orders, start, cosines, weights)


def apply_table(table, received, first):
    senders, _, rows, columns = received.shape
    slots, out_rows, _ = table.shape
    half = out_rows // 2

    def body(table_ref, data_ref, own_ref, other_ref, wide_ref):
        for s in range(slots):
            data = data_ref[:, first + s].reshape(senders * rows, columns)
            product = jnp.dot(table_ref[s], data, preferred_element_type=jnp.float32)
            own_ref[pl.ds(s, half, stride=slots), :] = product[:half]
            wide_ref[pl.ds(s, half, stride=slots), :] = product[half:]
        other_ref[...] = wide_ref[...].astype(jnp.bfloat16)

    return pl.pallas_call(
        body,
        out_shape=(
            whole((half * slots, columns), jnp.float32),
            whole((half * slots, columns), jnp.bfloat16),
        ),
        in_specs=[IN_VMEM] * 2,
        out_specs=(IN_VMEM, IN_VMEM),
        scratch_shapes=[pltpu.VMEM((half * slots, columns), jnp.float32)],
        compiler_params=params(6),
    )(table, received)


def slot_rows(offsets, ranks):
    return [offsets - s * ranks for s in range(GROUP)]


def spectral_part(analysis, received, ranks):
    senders, _, rows, columns = received.shape
    kept = slot_rows(analysis.shape[1], ranks)

    def body(table_ref, data_ref, own_ref, other_ref):
        parts = []
        for s in range(GROUP):
            data = data_ref[:, s].reshape(senders * rows, columns)
            product = jnp.dot(table_ref[s], data, preferred_element_type=jnp.float32)
            parts.append(product[: kept[s]])
        spectral = jnp.concatenate(parts, axis=0)
        own_ref[...] = spectral
        other_ref[...] = spectral.astype(jnp.bfloat16)

    shape = (sum(kept), columns)
    return pl.pallas_call(
        body,
        out_shape=(whole(shape, jnp.float32), whole(shape, jnp.bfloat16)),
        in_specs=[IN_VMEM] * 2,
        out_specs=[IN_VMEM] * 2,
        compiler_params=params(6),
    )(analysis, received)


def spectral_band(evaluation, own, mirrored, ranks):
    _, half, offsets = evaluation.shape
    columns = own.shape[1]
    kept = slot_rows(offsets, ranks)

    def body(table_ref, own_ref, mirrored_ref, out_ref, wide_ref):
        spectral = own_ref[...] + mirrored_ref[...].astype(jnp.float32)
        start = 0
        for s in range(GROUP):
            rows = spectral[start : start + kept[s]].astype(jnp.bfloat16)
            start += kept[s]
            product = jnp.dot(table_ref[s, :, : kept[s]], rows, preferred_element_type=jnp.float32)
            wide_ref[pl.ds(s, half, stride=GROUP), :] = product
        out_ref[...] = wide_ref[...].astype(jnp.bfloat16)

    return pl.pallas_call(
        body,
        out_shape=whole((half * GROUP, columns), jnp.bfloat16),
        in_specs=[IN_VMEM] * 3,
        out_specs=IN_VMEM,
        scratch_shapes=[pltpu.VMEM((half * GROUP, columns), jnp.float32)],
        compiler_params=params(6),
    )(evaluation, own, mirrored)


def grid_maxima(early, late, synthesis, labels, band_rows, fields, storm_count):
    ranks, early_rows, columns = early.shape
    rows, lon_count = labels.shape
    early_groups = early_rows // (band_rows * GROUP)
    groups = early_groups + 1
    waves = ranks * groups * GROUP
    wave_tiles = waves // LANES
    tiles = synthesis.shape[1] // LANES
    tail = lon_count - (tiles - 1) * LANES
    span = math.gcd(rows, 256)
    block = math.gcd(rows, 128)
    sets = [(t, r) for t in range(tiles) for r in range(0, rows, span)]

    def body(early_ref, late_ref, synthesis_ref, label_ref, filtered_ref, out_ref, *scratch):
        wide_ref, left_ref, kept_ref, tail_ref, top_ref = scratch
        tail_ref[...] = jnp.full(tail_ref.shape, storm_count, jnp.int32)
        tail_ref[:, 0:tail] = label_ref[:, lon_count - tail : lon_count]

        def names(t, row):
            if t == tiles - 1:
                return tail_ref[pl.ds(row, 8), :]
            return label_ref[pl.ds(row, 8), t * LANES : (t + 1) * LANES]

        for a in range(ranks):
            wide_ref[a, 0:early_rows] = early_ref[a].astype(jnp.float32)
            wide_ref[a, early_rows:] = late_ref[a].astype(jnp.float32)
        for o in range(band_rows):
            pieces = [
                wide_ref[a, (g * band_rows + o) * GROUP : (g * band_rows + o + 1) * GROUP]
                for a in range(ranks)
                for g in range(groups)
            ]
            turned = jnp.concatenate(pieces, axis=0).T
            for r in range(2):
                for w in range(wave_tiles):
                    left_ref[r * wave_tiles + w, pl.ds(o, fields, stride=band_rows), :] = turned[
                        r * fields : (r + 1) * fields, w * LANES : (w + 1) * LANES
                    ]
        for row in range(0, rows, block):
            left = [left_ref[i, row : row + block, :] for i in range(2 * wave_tiles)]
            left = jnp.concatenate(left, axis=1).astype(jnp.bfloat16)
            values = jnp.dot(left, synthesis_ref[...], preferred_element_type=jnp.float32)
            filtered_ref[row : row + block, :] = values[:, :lon_count].astype(jnp.bfloat16)
            for t in range(tiles):
                for i in range(0, block, 8):
                    kept_ref[t, row + i : row + i + 8, :] = jnp.where(
                        names(t, row + i) < storm_count,
                        values[i : i + 8, t * LANES : (t + 1) * LANES],
                        FLOOR,
                    )
        bests = []
        storms = []
        for t, start in sets:
            best = jnp.full((8, LANES), FLOOR, jnp.float32)
            storm = jnp.zeros((8, LANES), jnp.int32)
            for i in range(start, start + span, 8):
                value = kept_ref[t, i : i + 8, :]
                higher = value > best
                best = jnp.where(higher, value, best)
                storm = jnp.where(higher, names(t, i), storm)
            bests.append(best)
            storms.append(storm)

        def raise_tops(bests, storms):
            def per_storm(i, carry):
                picked = [jnp.where(storm == i, best, FLOOR) for best, storm in zip(bests, storms)]
                while len(picked) > 1:
                    paired = [jnp.maximum(a, b) for a, b in zip(picked[::2], picked[1::2])]
                    picked = paired + picked[2 * len(paired):]
                top = jnp.max(picked[0], axis=0, keepdims=True)
                top_ref[pl.ds(i, 1), :] = jnp.maximum(top_ref[pl.ds(i, 1), :], top)
                return carry

            lax.fori_loop(0, storm_count, per_storm, 0, unroll=8)

        def merge(a, b):
            higher = b[0] > a[0]
            return (jnp.where(higher, b[0], a[0]), jnp.where(higher, b[1], a[1]), a[2] + b[2])

        def tops():
            return jnp.max(top_ref[...].T, axis=0, keepdims=True)

        top_ref[...] = jnp.full(top_ref.shape, FLOOR, jnp.float32)
        raise_tops(bests, storms)

        def scan(carry):
            top = tops()
            table = [
                jnp.broadcast_to(top[:, h * LANES : (h + 1) * LANES], (8, LANES))
                for h in range(storm_count // LANES)
            ]
            tiny = jnp.zeros((8, LANES), jnp.float32)

            def per_rows(i, state):
                row = pl.multiple_of(i * (8 * SCAN_ROWS), 8 * SCAN_ROWS)
                merged = []
                for t in range(tiles):
                    found = [state[t]]
                    for r in range(SCAN_ROWS):
                        value = kept_ref[t, pl.ds(row + 8 * r, 8), :]
                        name = names(t, row + 8 * r)
                        place = jnp.bitwise_and(name, LANES - 1)
                        known = jnp.take_along_axis(table[0], place, axis=1)
                        for h in range(1, len(table)):
                            other = jnp.take_along_axis(table[h], place, axis=1)
                            known = jnp.where(name >= h * LANES, other, known)
                        is_open = value > known
                        found.append(
                            (
                                jnp.where(is_open, value, FLOOR),
                                name,
                                jnp.where(is_open, 1.0, 0.0),
                            )
                        )
                    while len(found) > 1:
                        paired = [merge(a, b) for a, b in zip(found[::2], found[1::2])]
                        found = paired + found[2 * len(paired) :]
                    merged.append(found[0])
                return tuple(merged)

            floor = jnp.full((8, LANES), FLOOR, jnp.float32)
            init = ((floor, jnp.zeros((8, LANES), jnp.int32), tiny),) * tiles
            state = lax.fori_loop(0, rows // (8 * SCAN_ROWS), per_rows, init)
            count = functools.reduce(jnp.maximum, [part[2] for part in state])
            most = jnp.max(count)

            @pl.when(most > 0.0)
            def _():
                raise_tops([part[0] for part in state], [part[1] for part in state])

            return most

        lax.while_loop(lambda most: most > 1.0, scan, jnp.float32(2.0))
        out_ref[...] = tops()

    return pl.pallas_call(
        body,
        out_shape=(whole((rows, lon_count), jnp.bfloat16), whole((1, storm_count), jnp.float32)),
        in_specs=[IN_VMEM] * 4,
        out_specs=(IN_VMEM, IN_VMEM),
        scratch_shapes=[
            pltpu.VMEM((ranks, groups * band_rows * GROUP, columns), jnp.float32),
            pltpu.VMEM((2 * wave_tiles, rows, LANES), jnp.float32),
            pltpu.VMEM((tiles, rows, LANES), jnp.float32),
            pltpu.VMEM((rows, LANES), jnp.int32),
            pltpu.VMEM((storm_count, LANES), jnp.float32),
        ],
        compiler_params=params(24),
    )(early, late, synthesis, labels)


def after(x, *others):
    return lax.optimization_barrier((x, *others))[0]


def local(vorticity, lat_order, storm_labels, storm_owner):
    field_count, lat_rows, lon_count = vorticity.shape
    lat_count = lat_order.shape[0]
    halves = lax.axis_size("half")
    ranks = lax.axis_size("rest")
    half_index = lax.axis_index("half")
    rank = lax.axis_index("rest")
    band_rows = storm_labels.shape[1]
    storm_count = storm_owner.shape[0]
    slots = MW // ranks
    chunks = slots // GROUP
    columns = 2 * field_count
    out_half = OUT_LAT // halves

    calls = [[16], [8, 8]] if slots == 32 else [[slots // 2], [slots // 2]]
    full_table = fourier_table(lon_count).reshape(lon_count, slots, ranks, 2)
    coefficients = []
    first = 0
    for part_slots in calls:
        pieces = []
        base = first
        for n in part_slots:
            pieces.append(full_table[:, base : base + n].transpose(0, 2, 1, 3).reshape(lon_count, -1, 2))
            base += n
        table = np.concatenate(pieces, axis=1).transpose(0, 2, 1).reshape(lon_count, -1)
        table = jnp.asarray(table.astype(jnp.bfloat16))
        coefficients += fourier(vorticity, table, ranks, part_slots)
        first = base
    stages = [n // GROUP for part_slots in calls for n in part_slots]
    group_count = slots // GROUP

    half_rows = ranks * lat_rows
    own_order = lax.dynamic_slice_in_dim(lat_order, half_index * half_rows, half_rows)
    colatitude = math.pi * (4.0 * own_order.astype(jnp.float32) + 3.0) / (4.0 * lat_count + 2.0)
    weights = math.pi / lat_count * jnp.sin(colatitude)
    band_index = jnp.arange(OUT_LAT, dtype=jnp.int32)
    band_index = ((band_index + half_index * out_half) % OUT_LAT).astype(jnp.float32)
    latitude = ((OUT_LAT - 1) / 2.0 - band_index) * (360.0 / OUT_LON) * (math.pi / 180.0)
    sine_values = jnp.concatenate([jnp.cos(latitude), jnp.sin(colatitude)])
    cosines = jnp.concatenate([jnp.sin(latitude), jnp.cos(colatitude)])
    orders = jnp.arange(slots, dtype=jnp.int32) * ranks + rank
    start_logs = jnp.asarray(diagonal_logs().reshape(slots, ranks))
    start_logs = lax.dynamic_slice_in_dim(start_logs, rank, 1, axis=1)
    orders = orders.astype(jnp.float32)[:, None]
    start = jnp.exp(start_logs + orders * jnp.log(sine_values)[None, :])
    def kernel(group, token):
        ordered = start if token is None else after(start, token)
        return kernel_table(
            orders[group * GROUP : (group + 1) * GROUP],
            ordered[group * GROUP : (group + 1) * GROUP],
            cosines[None, :],
            weights[None, :],
            OUT_LAT,
            MW - group * GROUP * ranks,
            out_half if group == group_count - 1 else 0,
        )

    def exchange(block):
        return lax.all_to_all(block, "rest", split_axis=0, concat_axis=0, tiled=True)

    def swapped(block):
        return lax.ppermute(block, "half", [(0, 1), (1, 0)])

    begins = [sum(stages[:i]) for i in range(len(stages) + 1)]
    last_stage = len(stages) - 1
    received = exchange(coefficients[0])
    tables = [kernel(0, coefficients[-1][0, 0, 0, :1])]
    cover = [coefficients[-1], *[part for table in tables for part in table]]
    swaps = []
    bands = []
    for i, count in enumerate(stages):
        received = after(received, *cover)
        if i == 1 and i < last_stage:
            received = after(received, swaps[0])
        following = None
        if i < last_stage:
            following = exchange(after(coefficients[i + 1], received))
        for g in range(begins[i], begins[i + 1]):
            if g == group_count - 1:
                own, other = spectral_part(tables[g][0], received, ranks)
                band = spectral_band(tables[g][1], own, swapped(other), ranks)
            else:
                own, other = apply_table(tables[g][0], received, (g - begins[i]) * GROUP)
                swaps.append(swapped(other))
                band = (own + swaps[-1].astype(jnp.float32)).astype(jnp.bfloat16)
            bands.append(band.reshape(ranks, band_rows * GROUP, columns))
            if i == 0 and g + 1 < stages[0]:
                tables.append(kernel(g + 1, other[0, :1]))
        if i == 0:
            later = [kernel(g, other[0, :1]) for g in range(stages[0], group_count)]
            tables += later
            cover = [other, *[part for table in later for part in table]]
        else:
            cover = [other, *bands]
        last_received, received = received, following

    early = exchange(after(jnp.concatenate(bands[:-1], axis=1), last_received))
    late = exchange(after(bands[-1], early))
    synthesis = synthesis_table(OUT_LON).reshape(group_count, GROUP, ranks, 2, OUT_LON)
    synthesis = synthesis.transpose(3, 2, 0, 1, 4).reshape(2 * MW, OUT_LON)
    synthesis = np.pad(synthesis, ((0, 0), (0, -OUT_LON % LANES)))
    filtered, local_peaks = grid_maxima(
        early,
        late,
        jnp.asarray(synthesis.astype(jnp.bfloat16)),
        storm_labels.reshape(field_count * band_rows, OUT_LON),
        band_rows,
        field_count,
        storm_count,
    )
    filtered = filtered.reshape(field_count, band_rows, OUT_LON)
    local_peaks = local_peaks[0]
    slot_ids = jnp.arange(storm_count, dtype=jnp.int32)
    by_slot = jnp.max(
        jnp.where(storm_owner[:, None] == slot_ids[None, :], local_peaks[:, None], FLOOR), axis=0
    )
    spec_count = halves * ranks
    shares = lax.all_to_all(
        by_slot.reshape(spec_count, storm_count // spec_count),
        ("half", "rest"),
        split_axis=0,
        concat_axis=0,
        tiled=True,
    )
    return (filtered, jnp.max(shares, axis=0))


def solution(mesh):
    groups = mesh.shape["grp"]
    spec_count = mesh.shape["spec"]
    split = Mesh(
        mesh.devices.reshape(groups, 2, spec_count // 2), axis_names=("grp", "half", "rest")
    )
    both = ("half", "rest")
    return jax.shard_map(
        local,
        mesh=split,
        in_specs=(P("grp", both, None), P(), P("grp", both, None), P("grp")),
        out_specs=(P("grp", both, None), P(("grp", "half", "rest"))),
        check_vma=False,
    )
```

```python
import functools
import math

import jax
import jax.numpy as jnp
import numpy as np
from jax import lax
from jax.experimental import pallas as pl
from jax.experimental.pallas import tpu as pltpu
from jax.sharding import Mesh
from jax.sharding import PartitionSpec as P

MW = 256
OUT_LAT = 256
OUT_LON = 720
FLOOR = -1e30
GROUP = 8
LANES = 128
SCAN_ROWS = 8


def fourier_table(lon_count):
    steps = np.arange(lon_count)[:, None] * np.arange(MW)[None, :] % lon_count
    angles = steps * (2.0 * math.pi / lon_count)
    return np.stack([np.cos(angles), -np.sin(angles)], axis=-1) / lon_count


def synthesis_table(lon_count):
    steps = np.arange(MW)[:, None] * np.arange(lon_count)[None, :] % lon_count
    angles = steps * (2.0 * math.pi / lon_count)
    factor = np.where(np.arange(MW) == 0, 1.0, 2.0)[:, None]
    return np.stack([factor * np.cos(angles), -factor * np.sin(angles)], axis=1)


def diagonal_logs():
    counters = np.arange(1, MW, dtype=np.float64)
    increments = np.log((2.0 * counters + 1.0) / (2.0 * counters))
    sums = np.concatenate([[0.0], np.cumsum(increments)])
    return (0.5 * math.log(0.5) + 0.5 * sums).astype(np.float32)


def params(mebibytes):
    return pltpu.CompilerParams(vmem_limit_bytes=mebibytes << 20)


def whole(shape, dtype):
    return jax.ShapeDtypeStruct(shape, dtype)


IN_VMEM = pl.BlockSpec(memory_space=pltpu.VMEM)


def fourier(vorticity, table, senders, part_slots):
    fields, rows, lon_count = vorticity.shape
    waves = table.shape[1] // 2
    block = 16 if rows % 16 == 0 else 8
    parts = len(part_slots)

    steps = rows // block

    def body(data_ref, table_ref, *refs):
        out_refs, (even_ref, odd_ref, turned_ref) = refs[:parts], refs[parts:]

        def multiply(product_ref):
            data = data_ref[...].reshape(fields * block, lon_count)
            product = jnp.dot(data, table_ref[...], preferred_element_type=jnp.float32)
            for t in range(2 * waves // LANES):
                product_ref[t] = product[:, t * LANES : (t + 1) * LANES]

        def turn(product_ref):
            for j in range(block):
                for t in range(waves // LANES):
                    pair = [
                        product_ref[r * (waves // LANES) + t, pl.ds(j, fields, stride=block), :]
                        for r in range(2)
                    ]
                    turned = jnp.concatenate(pair, axis=0).T
                    turned_ref[pl.ds(t * LANES * block + j, LANES, stride=block), :] = turned
            start = 0
            for p in range(parts):
                size = senders * part_slots[p] * block
                part = turned_ref[start : start + size, :]
                out_refs[p][...] = part.astype(jnp.bfloat16).reshape(out_refs[p].shape)
                start += size

        step = pl.program_id(0)
        buffers = (even_ref, odd_ref)

        @pl.when(step == 0)
        def _():
            multiply(even_ref)

        for parity in range(2):

            @pl.when((step > 0) & (step < steps) & (step % 2 == parity))
            def _():
                multiply(buffers[parity])
                turn(buffers[1 - parity])

        @pl.when(step == steps)
        def _():
            turn(buffers[(steps - 1) % 2])

    return pl.pallas_call(
        body,
        out_shape=[whole((senders, n, rows, 2 * fields), jnp.bfloat16) for n in part_slots],
        grid=(steps + 1,),
        in_specs=[
            pl.BlockSpec((fields, block, lon_count), lambda i: (0, jnp.minimum(i, steps - 1), 0)),
            pl.BlockSpec(table.shape, lambda i: (0, 0), pipeline_mode=pl.Buffered(1)),
        ],
        out_specs=[
            pl.BlockSpec((senders, n, block, 2 * fields), lambda i: (0, 0, jnp.maximum(i - 1, 0), 0)) for n in part_slots
        ],
        scratch_shapes=[
            pltpu.VMEM((2 * waves // LANES, fields * block, LANES), jnp.float32),
            pltpu.VMEM((2 * waves // LANES, fields * block, LANES), jnp.float32),
            pltpu.VMEM((waves * block, 2 * fields), jnp.float32),
        ],
        compiler_params=params(20),
    )(pltpu.with_memory_space_constraint(vorticity, pltpu.HBM), table)


def halves_of(x):
    high = x.astype(jnp.bfloat16)
    return high, (x - high.astype(jnp.float32)).astype(jnp.bfloat16)


def kernel_table(orders, start, cosines, weights, out_rows, offsets, split_rows):
    columns = start.shape[1]
    in_rows = columns - out_rows
    tiles = columns // LANES
    out_tiles = out_rows // LANES

    def body(order_ref, start_ref, cos_ref, weight_ref, *refs):
        out_refs, table_ref = refs[:-1], refs[-1]
        m = jnp.broadcast_to(order_ref[...], (GROUP, LANES))
        cosine = [
            jnp.broadcast_to(cos_ref[:, t * LANES : (t + 1) * LANES], (GROUP, LANES))
            for t in range(tiles)
        ]

        def step(k, carry):
            previous, earlier = carry
            offset = k.astype(jnp.float32)
            degree = m + offset
            below = degree - 1.0
            first = jnp.sqrt((4.0 * degree * degree - 1.0) / (offset * (2.0 * m + offset)))
            second = jnp.sqrt(
                (offset - 1.0)
                * (2.0 * m + offset - 1.0)
                / jnp.maximum(4.0 * below * below - 1.0, 1.0)
            )
            keep = degree <= MW - 1.0
            row = pl.multiple_of(k * GROUP, GROUP)
            current = []
            for t in range(tiles):
                value = first * (cosine[t] * previous[t] - second * earlier[t])
                current.append(value)
                stored = jnp.where(keep, value, 0.0) if t < out_tiles else value
                table_ref[t, pl.ds(row, GROUP), :] = stored
            return (tuple(current), previous)

        first_rows = tuple(start_ref[:, t * LANES : (t + 1) * LANES] for t in range(tiles))
        for t in range(tiles):
            table_ref[t, 0:GROUP, :] = first_rows[t]
        zeros = tuple(jnp.zeros((GROUP, LANES), jnp.float32) for _ in range(tiles))
        first_step = step(jnp.int32(1), (first_rows, zeros))
        second_step = step(jnp.int32(2), first_step)
        third_step = step(jnp.int32(3), second_step)
        lax.fori_loop(4, offsets, step, third_step, unroll=4)
        weight = weight_ref[...]
        for s in range(GROUP):
            values = [table_ref[t, pl.ds(s, offsets, stride=GROUP), :] for t in range(tiles)]
            if split_rows:
                inward = jnp.concatenate(values[out_tiles:], axis=1) * weight
                out_refs[0][s] = inward.astype(jnp.bfloat16)
                outward = jnp.concatenate(values[: split_rows // LANES], axis=1)
                out_refs[1][s] = outward.T.astype(jnp.bfloat16)
                continue
            out_high, out_low = halves_of(jnp.concatenate(values[:out_tiles], axis=1))
            in_high, in_low = halves_of(jnp.concatenate(values[out_tiles:], axis=1))
            product = lax.dot_general(
                jnp.concatenate([out_high, out_high, out_low], axis=0),
                jnp.concatenate([in_high, in_low, in_high], axis=0),
                (((0,), (0,)), ((), ())),
                preferred_element_type=jnp.float32,
            )
            out_refs[0][s] = (product * weight).astype(jnp.bfloat16)

    out_shape = [whole((GROUP, out_rows, in_rows), jnp.bfloat16)]
    if split_rows:
        out_shape = [
            whole((GROUP, offsets, in_rows), jnp.bfloat16),
            whole((GROUP, split_rows, offsets), jnp.bfloat16),
        ]
    return pl.pallas_call(
        body,
        out_shape=out_shape,
        in_specs=[IN_VMEM] * 4,
        out_specs=[IN_VMEM] * len(out_shape),
        scratch_shapes=[pltpu.VMEM((tiles, offsets * GROUP, LANES), jnp.float32)],
        compiler_params=params(14),
    )(orders, start, cosines, weights)


def apply_table(table, received, first):
    senders, _, rows, columns = received.shape
    slots, out_rows, _ = table.shape
    half = out_rows // 2

    def body(table_ref, data_ref, own_ref, other_ref, wide_ref):
        for s in range(slots):
            data = data_ref[:, first + s].reshape(senders * rows, columns)
            product = jnp.dot(table_ref[s], data, preferred_element_type=jnp.float32)
            own_ref[pl.ds(s, half, stride=slots), :] = product[:half]
            wide_ref[pl.ds(s, half, stride=slots), :] = product[half:]
        other_ref[...] = wide_ref[...].astype(jnp.bfloat16)

    return pl.pallas_call(
        body,
        out_shape=(
            whole((half * slots, columns), jnp.float32),
            whole((half * slots, columns), jnp.bfloat16),
        ),
        in_specs=[IN_VMEM] * 2,
        out_specs=(IN_VMEM, IN_VMEM),
        scratch_shapes=[pltpu.VMEM((half * slots, columns), jnp.float32)],
        compiler_params=params(6),
    )(table, received)


def slot_rows(offsets, ranks):
    return [offsets - s * ranks for s in range(GROUP)]


def spectral_part(analysis, received, ranks):
    senders, _, rows, columns = received.shape
    kept = slot_rows(analysis.shape[1], ranks)

    def body(table_ref, data_ref, own_ref, other_ref):
        parts = []
        for s in range(GROUP):
            data = data_ref[:, s].reshape(senders * rows, columns)
            product = jnp.dot(table_ref[s], data, preferred_element_type=jnp.float32)
            parts.append(product[: kept[s]])
        spectral = jnp.concatenate(parts, axis=0)
        own_ref[...] = spectral
        other_ref[...] = spectral.astype(jnp.bfloat16)

    shape = (sum(kept), columns)
    return pl.pallas_call(
        body,
        out_shape=(whole(shape, jnp.float32), whole(shape, jnp.bfloat16)),
        in_specs=[IN_VMEM] * 2,
        out_specs=[IN_VMEM] * 2,
        compiler_params=params(6),
    )(analysis, received)


def spectral_band(evaluation, own, mirrored, ranks):
    _, half, offsets = evaluation.shape
    columns = own.shape[1]
    kept = slot_rows(offsets, ranks)

    def body(table_ref, own_ref, mirrored_ref, out_ref, wide_ref):
        spectral = own_ref[...] + mirrored_ref[...].astype(jnp.float32)
        start = 0
        for s in range(GROUP):
            rows = spectral[start : start + kept[s]].astype(jnp.bfloat16)
            start += kept[s]
            product = jnp.dot(table_ref[s, :, : kept[s]], rows, preferred_element_type=jnp.float32)
            wide_ref[pl.ds(s, half, stride=GROUP), :] = product
        out_ref[...] = wide_ref[...].astype(jnp.bfloat16)

    return pl.pallas_call(
        body,
        out_shape=whole((half * GROUP, columns), jnp.bfloat16),
        in_specs=[IN_VMEM] * 3,
        out_specs=IN_VMEM,
        scratch_shapes=[pltpu.VMEM((half * GROUP, columns), jnp.float32)],
        compiler_params=params(6),
    )(evaluation, own, mirrored)


def grid_maxima(early, late, synthesis, labels, band_rows, fields, storm_count):
    ranks, early_rows, columns = early.shape
    rows, lon_count = labels.shape
    early_groups = early_rows // (band_rows * GROUP)
    groups = early_groups + 1
    waves = ranks * groups * GROUP
    wave_tiles = waves // LANES
    tiles = synthesis.shape[1] // LANES
    tail = lon_count - (tiles - 1) * LANES
    span = math.gcd(rows, 256)
    block = math.gcd(rows, 128)
    sets = [(t, r) for t in range(tiles) for r in range(0, rows, span)]

    def body(early_ref, late_ref, synthesis_ref, label_ref, filtered_ref, out_ref, *scratch):
        wide_ref, left_ref, kept_ref, tail_ref, top_ref = scratch
        tail_ref[...] = jnp.full(tail_ref.shape, storm_count, jnp.int32)
        tail_ref[:, 0:tail] = label_ref[:, lon_count - tail : lon_count]

        def names(t, row):
            if t == tiles - 1:
                return tail_ref[pl.ds(row, 8), :]
            return label_ref[pl.ds(row, 8), t * LANES : (t + 1) * LANES]

        for a in range(ranks):
            wide_ref[a, 0:early_rows] = early_ref[a].astype(jnp.float32)
            wide_ref[a, early_rows:] = late_ref[a].astype(jnp.float32)
        for o in range(band_rows):
            pieces = [
                wide_ref[a, (g * band_rows + o) * GROUP : (g * band_rows + o + 1) * GROUP]
                for a in range(ranks)
                for g in range(groups)
            ]
            turned = jnp.concatenate(pieces, axis=0).T
            for r in range(2):
                for w in range(wave_tiles):
                    left_ref[r * wave_tiles + w, pl.ds(o, fields, stride=band_rows), :] = turned[
                        r * fields : (r + 1) * fields, w * LANES : (w + 1) * LANES
                    ]
        for row in range(0, rows, block):
            left = [left_ref[i, row : row + block, :] for i in range(2 * wave_tiles)]
            left = jnp.concatenate(left, axis=1).astype(jnp.bfloat16)
            values = jnp.dot(left, synthesis_ref[...], preferred_element_type=jnp.float32)
            filtered_ref[row : row + block, :] = values[:, :lon_count].astype(jnp.bfloat16)
            for t in range(tiles):
                for i in range(0, block, 8):
                    kept_ref[t, row + i : row + i + 8, :] = jnp.where(
                        names(t, row + i) < storm_count,
                        values[i : i + 8, t * LANES : (t + 1) * LANES],
                        FLOOR,
                    )
        bests = []
        storms = []
        for t, start in sets:
            best = jnp.full((8, LANES), FLOOR, jnp.float32)
            storm = jnp.zeros((8, LANES), jnp.int32)
            for i in range(start, start + span, 8):
                value = kept_ref[t, i : i + 8, :]
                higher = value > best
                best = jnp.where(higher, value, best)
                storm = jnp.where(higher, names(t, i), storm)
            bests.append(best)
            storms.append(storm)

        def raise_tops(bests, storms):
            def per_storm(i, carry):
                picked = [jnp.where(storm == i, best, FLOOR) for best, storm in zip(bests, storms)]
                while len(picked) > 1:
                    paired = [jnp.maximum(a, b) for a, b in zip(picked[::2], picked[1::2])]
                    picked = paired + picked[2 * len(paired):]
                top = jnp.max(picked[0], axis=0, keepdims=True)
                top_ref[pl.ds(i, 1), :] = jnp.maximum(top_ref[pl.ds(i, 1), :], top)
                return carry

            lax.fori_loop(0, storm_count, per_storm, 0, unroll=8)

        def merge(a, b):
            higher = b[0] > a[0]
            return (jnp.where(higher, b[0], a[0]), jnp.where(higher, b[1], a[1]), a[2] + b[2])

        def tops():
            return jnp.max(top_ref[...].T, axis=0, keepdims=True)

        top_ref[...] = jnp.full(top_ref.shape, FLOOR, jnp.float32)
        raise_tops(bests, storms)

        def scan(carry):
            top = tops()
            table = [
                jnp.broadcast_to(top[:, h * LANES : (h + 1) * LANES], (8, LANES))
                for h in range(storm_count // LANES)
            ]
            tiny = jnp.zeros((8, LANES), jnp.float32)

            def per_rows(i, state):
                row = pl.multiple_of(i * (8 * SCAN_ROWS), 8 * SCAN_ROWS)
                merged = []
                for t in range(tiles):
                    found = [state[t]]
                    for r in range(SCAN_ROWS):
                        value = kept_ref[t, pl.ds(row + 8 * r, 8), :]
                        name = names(t, row + 8 * r)
                        place = jnp.bitwise_and(name, LANES - 1)
                        known = jnp.take_along_axis(table[0], place, axis=1)
                        for h in range(1, len(table)):
                            other = jnp.take_along_axis(table[h], place, axis=1)
                            known = jnp.where(name >= h * LANES, other, known)
                        is_open = value > known
                        found.append(
                            (
                                jnp.where(is_open, value, FLOOR),
                                name,
                                jnp.where(is_open, 1.0, 0.0),
                            )
                        )
                    while len(found) > 1:
                        paired = [merge(a, b) for a, b in zip(found[::2], found[1::2])]
                        found = paired + found[2 * len(paired) :]
                    merged.append(found[0])
                return tuple(merged)

            floor = jnp.full((8, LANES), FLOOR, jnp.float32)
            init = ((floor, jnp.zeros((8, LANES), jnp.int32), tiny),) * tiles
            state = lax.fori_loop(0, rows // (8 * SCAN_ROWS), per_rows, init)
            count = functools.reduce(jnp.maximum, [part[2] for part in state])
            most = jnp.max(count)

            @pl.when(most > 0.0)
            def _():
                raise_tops([part[0] for part in state], [part[1] for part in state])

            return most

        lax.while_loop(lambda most: most > 1.0, scan, jnp.float32(2.0))
        out_ref[...] = tops()

    return pl.pallas_call(
        body,
        out_shape=(whole((rows, lon_count), jnp.bfloat16), whole((1, storm_count), jnp.float32)),
        in_specs=[IN_VMEM] * 4,
        out_specs=(IN_VMEM, IN_VMEM),
        scratch_shapes=[
            pltpu.VMEM((ranks, groups * band_rows * GROUP, columns), jnp.float32),
            pltpu.VMEM((2 * wave_tiles, rows, LANES), jnp.float32),
            pltpu.VMEM((tiles, rows, LANES), jnp.float32),
            pltpu.VMEM((rows, LANES), jnp.int32),
            pltpu.VMEM((storm_count, LANES), jnp.float32),
        ],
        compiler_params=params(24),
    )(early, late, synthesis, labels)


def after(x, *others):
    return lax.optimization_barrier((x, *others))[0]


def local(vorticity, lat_order, storm_labels, storm_owner):
    field_count, lat_rows, lon_count = vorticity.shape
    lat_count = lat_order.shape[0]
    halves = lax.axis_size("half")
    ranks = lax.axis_size("rest")
    half_index = lax.axis_index("half")
    rank = lax.axis_index("rest")
    band_rows = storm_labels.shape[1]
    storm_count = storm_owner.shape[0]
    slots = MW // ranks
    chunks = slots // GROUP
    columns = 2 * field_count
    out_half = OUT_LAT // halves

    calls = [[16], [8, 8]] if slots == 32 else [[slots // 2], [slots // 2]]
    full_table = fourier_table(lon_count).reshape(lon_count, slots, ranks, 2)
    coefficients = []
    first = 0
    for part_slots in calls:
        pieces = []
        base = first
        for n in part_slots:
            pieces.append(full_table[:, base : base + n].transpose(0, 2, 1, 3).reshape(lon_count, -1, 2))
            base += n
        table = np.concatenate(pieces, axis=1).transpose(0, 2, 1).reshape(lon_count, -1)
        table = jnp.asarray(table.astype(jnp.bfloat16))
        coefficients += fourier(vorticity, table, ranks, part_slots)
        first = base
    stages = [n // GROUP for part_slots in calls for n in part_slots]
    group_count = slots // GROUP

    half_rows = ranks * lat_rows
    own_order = lax.dynamic_slice_in_dim(lat_order, half_index * half_rows, half_rows)
    colatitude = math.pi * (4.0 * own_order.astype(jnp.float32) + 3.0) / (4.0 * lat_count + 2.0)
    weights = math.pi / lat_count * jnp.sin(colatitude)
    band_index = jnp.arange(OUT_LAT, dtype=jnp.int32)
    band_index = ((band_index + half_index * out_half) % OUT_LAT).astype(jnp.float32)
    latitude = ((OUT_LAT - 1) / 2.0 - band_index) * (360.0 / OUT_LON) * (math.pi / 180.0)
    sine_values = jnp.concatenate([jnp.cos(latitude), jnp.sin(colatitude)])
    cosines = jnp.concatenate([jnp.sin(latitude), jnp.cos(colatitude)])
    orders = jnp.arange(slots, dtype=jnp.int32) * ranks + rank
    start_logs = jnp.asarray(diagonal_logs().reshape(slots, ranks))
    start_logs = lax.dynamic_slice_in_dim(start_logs, rank, 1, axis=1)
    orders = orders.astype(jnp.float32)[:, None]
    start = jnp.exp(start_logs + orders * jnp.log(sine_values)[None, :])
    def kernel(group, token):
        ordered = start if token is None else after(start, token)
        return kernel_table(
            orders[group * GROUP : (group + 1) * GROUP],
            ordered[group * GROUP : (group + 1) * GROUP],
            cosines[None, :],
            weights[None, :],
            OUT_LAT,
            MW - group * GROUP * ranks,
            out_half if group == group_count - 1 else 0,
        )

    def exchange(block):
        return lax.all_to_all(block, "rest", split_axis=0, concat_axis=0, tiled=True)

    def swapped(block):
        return lax.ppermute(block, "half", [(0, 1), (1, 0)])

    begins = [sum(stages[:i]) for i in range(len(stages) + 1)]
    last_stage = len(stages) - 1
    received = exchange(coefficients[0])
    tables = [kernel(0, coefficients[-1][0, 0, 0, :1])]
    cover = [coefficients[-1], *[part for table in tables for part in table]]
    swaps = []
    bands = []
    for i, count in enumerate(stages):
        received = after(received, *cover)
        if i == 1 and i < last_stage:
            received = after(received, swaps[0])
        following = None
        if i < last_stage:
            following = exchange(after(coefficients[i + 1], received))
        for g in range(begins[i], begins[i + 1]):
            if g == group_count - 1:
                own, other = spectral_part(tables[g][0], received, ranks)
                band = spectral_band(tables[g][1], own, swapped(other), ranks)
            else:
                own, other = apply_table(tables[g][0], received, (g - begins[i]) * GROUP)
                swaps.append(swapped(other))
                band = (own + swaps[-1].astype(jnp.float32)).astype(jnp.bfloat16)
            bands.append(band.reshape(ranks, band_rows * GROUP, columns))
            if i == 0 and g + 1 < stages[0]:
                tables.append(kernel(g + 1, other[0, :1]))
        if i == 0:
            later = [kernel(g, other[0, :1]) for g in range(stages[0], group_count)]
            tables += later
            cover = [other, *[part for table in later for part in table]]
        else:
            cover = [other, *bands]
        last_received, received = received, following

    early = exchange(after(jnp.concatenate(bands[:-1], axis=1), last_received))
    late = exchange(after(bands[-1], early))
    synthesis = synthesis_table(OUT_LON).reshape(group_count, GROUP, ranks, 2, OUT_LON)
    synthesis = synthesis.transpose(3, 2, 0, 1, 4).reshape(2 * MW, OUT_LON)
    synthesis = np.pad(synthesis, ((0, 0), (0, -OUT_LON % LANES)))
    filtered, local_peaks = grid_maxima(
        early,
        late,
        jnp.asarray(synthesis.astype(jnp.bfloat16)),
        storm_labels.reshape(field_count * band_rows, OUT_LON),
        band_rows,
        field_count,
        storm_count,
    )
    filtered = filtered.reshape(field_count, band_rows, OUT_LON)
    local_peaks = local_peaks[0]
    slot_ids = jnp.arange(storm_count, dtype=jnp.int32)
    by_slot = jnp.max(
        jnp.where(storm_owner[:, None] == slot_ids[None, :], local_peaks[:, None], FLOOR), axis=0
    )
    spec_count = halves * ranks
    shares = lax.all_to_all(
        by_slot.reshape(spec_count, storm_count // spec_count),
        ("half", "rest"),
        split_axis=0,
        concat_axis=0,
        tiled=True,
    )
    return (filtered, jnp.max(shares, axis=0))


def solution(mesh):
    groups = mesh.shape["grp"]
    spec_count = mesh.shape["spec"]
    split = Mesh(
        mesh.devices.reshape(groups, 2, spec_count // 2), axis_names=("grp", "half", "rest")
    )
    both = ("half", "rest")
    return jax.shard_map(
        local,
        mesh=split,
        in_specs=(P("grp", both, None), P(), P("grp", both, None), P("grp")),
        out_specs=(P("grp", both, None), P(("grp", "half", "rest"))),
        check_vma=False,
    )
```

```python
import functools
import math

import jax
import jax.numpy as jnp
import numpy as np
from jax import lax
from jax.experimental import pallas as pl
from jax.experimental.pallas import tpu as pltpu
from jax.sharding import Mesh
from jax.sharding import PartitionSpec as P

MW = 256
OUT_LAT = 256
OUT_LON = 720
FLOOR = -1e30
GROUP = 8
LANES = 128
SCAN_ROWS = 8


def fourier_table(lon_count):
    steps = np.arange(lon_count)[:, None] * np.arange(MW)[None, :] % lon_count
    angles = steps * (2.0 * math.pi / lon_count)
    return np.stack([np.cos(angles), -np.sin(angles)], axis=-1) / lon_count


def synthesis_table(lon_count):
    steps = np.arange(MW)[:, None] * np.arange(lon_count)[None, :] % lon_count
    angles = steps * (2.0 * math.pi / lon_count)
    factor = np.where(np.arange(MW) == 0, 1.0, 2.0)[:, None]
    return np.stack([factor * np.cos(angles), -factor * np.sin(angles)], axis=1)


def diagonal_logs():
    counters = np.arange(1, MW, dtype=np.float64)
    increments = np.log((2.0 * counters + 1.0) / (2.0 * counters))
    sums = np.concatenate([[0.0], np.cumsum(increments)])
    return (0.5 * math.log(0.5) + 0.5 * sums).astype(np.float32)


def params(mebibytes):
    return pltpu.CompilerParams(vmem_limit_bytes=mebibytes << 20)


def whole(shape, dtype):
    return jax.ShapeDtypeStruct(shape, dtype)


IN_VMEM = pl.BlockSpec(memory_space=pltpu.VMEM)


def fourier(vorticity, table, senders, part_slots):
    fields, rows, lon_count = vorticity.shape
    waves = table.shape[1] // 2
    block = 16 if rows % 16 == 0 else 8
    parts = len(part_slots)

    steps = rows // block

    def body(data_ref, table_ref, *refs):
        out_refs, (even_ref, odd_ref, turned_ref) = refs[:parts], refs[parts:]

        def multiply(product_ref):
            data = data_ref[...].reshape(fields * block, lon_count)
            product = jnp.dot(data, table_ref[...], preferred_element_type=jnp.float32)
            for t in range(2 * waves // LANES):
                product_ref[t] = product[:, t * LANES : (t + 1) * LANES]

        def turn(product_ref):
            for j in range(block):
                for t in range(waves // LANES):
                    pair = [
                        product_ref[r * (waves // LANES) + t, pl.ds(j, fields, stride=block), :]
                        for r in range(2)
                    ]
                    turned = jnp.concatenate(pair, axis=0).T
                    turned_ref[pl.ds(t * LANES * block + j, LANES, stride=block), :] = turned
            start = 0
            for p in range(parts):
                size = senders * part_slots[p] * block
                part = turned_ref[start : start + size, :]
                out_refs[p][...] = part.astype(jnp.bfloat16).reshape(out_refs[p].shape)
                start += size

        step = pl.program_id(0)
        buffers = (even_ref, odd_ref)

        @pl.when(step == 0)
        def _():
            multiply(even_ref)

        for parity in range(2):

            @pl.when((step > 0) & (step < steps) & (step % 2 == parity))
            def _():
                multiply(buffers[parity])
                turn(buffers[1 - parity])

        @pl.when(step == steps)
        def _():
            turn(buffers[(steps - 1) % 2])

    return pl.pallas_call(
        body,
        out_shape=[whole((senders, n, rows, 2 * fields), jnp.bfloat16) for n in part_slots],
        grid=(steps + 1,),
        in_specs=[
            pl.BlockSpec((fields, block, lon_count), lambda i: (0, jnp.minimum(i, steps - 1), 0)),
            pl.BlockSpec(table.shape, lambda i: (0, 0), pipeline_mode=pl.Buffered(1)),
        ],
        out_specs=[
            pl.BlockSpec((senders, n, block, 2 * fields), lambda i: (0, 0, jnp.maximum(i - 1, 0), 0)) for n in part_slots
        ],
        scratch_shapes=[
            pltpu.VMEM((2 * waves // LANES, fields * block, LANES), jnp.float32),
            pltpu.VMEM((2 * waves // LANES, fields * block, LANES), jnp.float32),
            pltpu.VMEM((waves * block, 2 * fields), jnp.float32),
        ],
        compiler_params=params(20),
    )(pltpu.with_memory_space_constraint(vorticity, pltpu.HBM), table)


def halves_of(x):
    high = x.astype(jnp.bfloat16)
    return high, (x - high.astype(jnp.float32)).astype(jnp.bfloat16)


def kernel_table(orders, start, cosines, weights, out_rows, offsets, split_rows):
    columns = start.shape[1]
    in_rows = columns - out_rows
    tiles = columns // LANES
    out_tiles = out_rows // LANES

    def body(order_ref, start_ref, cos_ref, weight_ref, *refs):
        out_refs, table_ref = refs[:-1], refs[-1]
        m = jnp.broadcast_to(order_ref[...], (GROUP, LANES))
        cosine = [
            jnp.broadcast_to(cos_ref[:, t * LANES : (t + 1) * LANES], (GROUP, LANES))
            for t in range(tiles)
        ]

        def step(k, carry):
            previous, earlier = carry
            offset = k.astype(jnp.float32)
            degree = m + offset
            below = degree - 1.0
            first = jnp.sqrt((4.0 * degree * degree - 1.0) / (offset * (2.0 * m + offset)))
            second = jnp.sqrt(
                (offset - 1.0)
                * (2.0 * m + offset - 1.0)
                / jnp.maximum(4.0 * below * below - 1.0, 1.0)
            )
            keep = degree <= MW - 1.0
            row = pl.multiple_of(k * GROUP, GROUP)
            current = []
            for t in range(tiles):
                value = first * (cosine[t] * previous[t] - second * earlier[t])
                current.append(value)
                stored = jnp.where(keep, value, 0.0) if t < out_tiles else value
                table_ref[t, pl.ds(row, GROUP), :] = stored
            return (tuple(current), previous)

        first_rows = tuple(start_ref[:, t * LANES : (t + 1) * LANES] for t in range(tiles))
        for t in range(tiles):
            table_ref[t, 0:GROUP, :] = first_rows[t]
        zeros = tuple(jnp.zeros((GROUP, LANES), jnp.float32) for _ in range(tiles))
        first_step = step(jnp.int32(1), (first_rows, zeros))
        second_step = step(jnp.int32(2), first_step)
        third_step = step(jnp.int32(3), second_step)
        lax.fori_loop(4, offsets, step, third_step, unroll=4)
        weight = weight_ref[...]
        for s in range(GROUP):
            values = [table_ref[t, pl.ds(s, offsets, stride=GROUP), :] for t in range(tiles)]
            if split_rows:
                inward = jnp.concatenate(values[out_tiles:], axis=1) * weight
                out_refs[0][s] = inward.astype(jnp.bfloat16)
                outward = jnp.concatenate(values[: split_rows // LANES], axis=1)
                out_refs[1][s] = outward.T.astype(jnp.bfloat16)
                continue
            out_high, out_low = halves_of(jnp.concatenate(values[:out_tiles], axis=1))
            in_high, in_low = halves_of(jnp.concatenate(values[out_tiles:], axis=1))
            product = lax.dot_general(
                jnp.concatenate([out_high, out_high, out_low], axis=0),
                jnp.concatenate([in_high, in_low, in_high], axis=0),
                (((0,), (0,)), ((), ())),
                preferred_element_type=jnp.float32,
            )
            out_refs[0][s] = (product * weight).astype(jnp.bfloat16)

    out_shape = [whole((GROUP, out_rows, in_rows), jnp.bfloat16)]
    if split_rows:
        out_shape = [
            whole((GROUP, offsets, in_rows), jnp.bfloat16),
            whole((GROUP, split_rows, offsets), jnp.bfloat16),
        ]
    return pl.pallas_call(
        body,
        out_shape=out_shape,
        in_specs=[IN_VMEM] * 4,
        out_specs=[IN_VMEM] * len(out_shape),
        scratch_shapes=[pltpu.VMEM((tiles, offsets * GROUP, LANES), jnp.float32)],
        compiler_params=params(14),
    )(orders, start, cosines, weights)


def apply_table(table, received, first):
    senders, _, rows, columns = received.shape
    slots, out_rows, _ = table.shape
    half = out_rows // 2

    def body(table_ref, data_ref, own_ref, other_ref, wide_ref):
        for s in range(slots):
            data = data_ref[:, first + s].reshape(senders * rows, columns)
            product = jnp.dot(table_ref[s], data, preferred_element_type=jnp.float32)
            own_ref[pl.ds(s, half, stride=slots), :] = product[:half]
            wide_ref[pl.ds(s, half, stride=slots), :] = product[half:]
        other_ref[...] = wide_ref[...].astype(jnp.bfloat16)

    return pl.pallas_call(
        body,
        out_shape=(
            whole((half * slots, columns), jnp.float32),
            whole((half * slots, columns), jnp.bfloat16),
        ),
        in_specs=[IN_VMEM] * 2,
        out_specs=(IN_VMEM, IN_VMEM),
        scratch_shapes=[pltpu.VMEM((half * slots, columns), jnp.float32)],
        compiler_params=params(6),
    )(table, received)


def slot_rows(offsets, ranks):
    return [offsets - s * ranks for s in range(GROUP)]


def spectral_part(analysis, received, ranks):
    senders, _, rows, columns = received.shape
    kept = slot_rows(analysis.shape[1], ranks)

    def body(table_ref, data_ref, own_ref, other_ref):
        parts = []
        for s in range(GROUP):
            data = data_ref[:, s].reshape(senders * rows, columns)
            product = jnp.dot(table_ref[s], data, preferred_element_type=jnp.float32)
            parts.append(product[: kept[s]])
        spectral = jnp.concatenate(parts, axis=0)
        own_ref[...] = spectral
        other_ref[...] = spectral.astype(jnp.bfloat16)

    shape = (sum(kept), columns)
    return pl.pallas_call(
        body,
        out_shape=(whole(shape, jnp.float32), whole(shape, jnp.bfloat16)),
        in_specs=[IN_VMEM] * 2,
        out_specs=[IN_VMEM] * 2,
        compiler_params=params(6),
    )(analysis, received)


def spectral_band(evaluation, own, mirrored, ranks):
    _, half, offsets = evaluation.shape
    columns = own.shape[1]
    kept = slot_rows(offsets, ranks)

    def body(table_ref, own_ref, mirrored_ref, out_ref, wide_ref):
        spectral = own_ref[...] + mirrored_ref[...].astype(jnp.float32)
        start = 0
        for s in range(GROUP):
            rows = spectral[start : start + kept[s]].astype(jnp.bfloat16)
            start += kept[s]
            product = jnp.dot(table_ref[s, :, : kept[s]], rows, preferred_element_type=jnp.float32)
            wide_ref[pl.ds(s, half, stride=GROUP), :] = product
        out_ref[...] = wide_ref[...].astype(jnp.bfloat16)

    return pl.pallas_call(
        body,
        out_shape=whole((half * GROUP, columns), jnp.bfloat16),
        in_specs=[IN_VMEM] * 3,
        out_specs=IN_VMEM,
        scratch_shapes=[pltpu.VMEM((half * GROUP, columns), jnp.float32)],
        compiler_params=params(6),
    )(evaluation, own, mirrored)


def grid_maxima(early, late, synthesis, labels, band_rows, fields, storm_count):
    ranks, early_rows, columns = early.shape
    rows, lon_count = labels.shape
    early_groups = early_rows // (band_rows * GROUP)
    groups = early_groups + 1
    waves = ranks * groups * GROUP
    wave_tiles = waves // LANES
    tiles = synthesis.shape[1] // LANES
    tail = lon_count - (tiles - 1) * LANES
    span = math.gcd(rows, 256)
    block = math.gcd(rows, 128)
    sets = [(t, r) for t in range(tiles) for r in range(0, rows, span)]

    def body(early_ref, late_ref, synthesis_ref, label_ref, filtered_ref, out_ref, *scratch):
        wide_ref, left_ref, kept_ref, tail_ref, top_ref = scratch
        tail_ref[...] = jnp.full(tail_ref.shape, storm_count, jnp.int32)
        tail_ref[:, 0:tail] = label_ref[:, lon_count - tail : lon_count]

        def names(t, row):
            if t == tiles - 1:
                return tail_ref[pl.ds(row, 8), :]
            return label_ref[pl.ds(row, 8), t * LANES : (t + 1) * LANES]

        for a in range(ranks):
            wide_ref[a, 0:early_rows] = early_ref[a].astype(jnp.float32)
            wide_ref[a, early_rows:] = late_ref[a].astype(jnp.float32)
        for o in range(band_rows):
            pieces = [
                wide_ref[a, (g * band_rows + o) * GROUP : (g * band_rows + o + 1) * GROUP]
                for a in range(ranks)
                for g in range(groups)
            ]
            turned = jnp.concatenate(pieces, axis=0).T
            for r in range(2):
                for w in range(wave_tiles):
                    left_ref[r * wave_tiles + w, pl.ds(o, fields, stride=band_rows), :] = turned[
                        r * fields : (r + 1) * fields, w * LANES : (w + 1) * LANES
                    ]
        for row in range(0, rows, block):
            left = [left_ref[i, row : row + block, :] for i in range(2 * wave_tiles)]
            left = jnp.concatenate(left, axis=1).astype(jnp.bfloat16)
            values = jnp.dot(left, synthesis_ref[...], preferred_element_type=jnp.float32)
            filtered_ref[row : row + block, :] = values[:, :lon_count].astype(jnp.bfloat16)
            for t in range(tiles):
                for i in range(0, block, 8):
                    kept_ref[t, row + i : row + i + 8, :] = jnp.where(
                        names(t, row + i) < storm_count,
                        values[i : i + 8, t * LANES : (t + 1) * LANES],
                        FLOOR,
                    )
        bests = []
        storms = []
        for t, start in sets:
            best = jnp.full((8, LANES), FLOOR, jnp.float32)
            storm = jnp.zeros((8, LANES), jnp.int32)
            for i in range(start, start + span, 8):
                value = kept_ref[t, i : i + 8, :]
                higher = value > best
                best = jnp.where(higher, value, best)
                storm = jnp.where(higher, names(t, i), storm)
            bests.append(best)
            storms.append(storm)

        def raise_tops(bests, storms):
            def per_storm(i, carry):
                picked = [jnp.where(storm == i, best, FLOOR) for best, storm in zip(bests, storms)]
                while len(picked) > 1:
                    paired = [jnp.maximum(a, b) for a, b in zip(picked[::2], picked[1::2])]
                    picked = paired + picked[2 * len(paired):]
                top = jnp.max(picked[0], axis=0, keepdims=True)
                top_ref[pl.ds(i, 1), :] = jnp.maximum(top_ref[pl.ds(i, 1), :], top)
                return carry

            lax.fori_loop(0, storm_count, per_storm, 0, unroll=8)

        def merge(a, b):
            higher = b[0] > a[0]
            return (jnp.where(higher, b[0], a[0]), jnp.where(higher, b[1], a[1]), a[2] + b[2])

        def tops():
            return jnp.max(top_ref[...].T, axis=0, keepdims=True)

        top_ref[...] = jnp.full(top_ref.shape, FLOOR, jnp.float32)
        raise_tops(bests, storms)

        def scan(carry):
            top = tops()
            table = [
                jnp.broadcast_to(top[:, h * LANES : (h + 1) * LANES], (8, LANES))
                for h in range(storm_count // LANES)
            ]
            tiny = jnp.zeros((8, LANES), jnp.float32)

            def per_rows(i, state):
                row = pl.multiple_of(i * (8 * SCAN_ROWS), 8 * SCAN_ROWS)
                merged = []
                for t, h in [(t, h) for t in range(tiles) for h in range(2)]:
                    found = [state[2 * t + h]]
                    for r in range(h, SCAN_ROWS, 2):
                        value = kept_ref[t, pl.ds(row + 8 * r, 8), :]
                        name = names(t, row + 8 * r)
                        place = jnp.bitwise_and(name, LANES - 1)
                        known = jnp.take_along_axis(table[0], place, axis=1)
                        for n in range(1, len(table)):
                            other = jnp.take_along_axis(table[n], place, axis=1)
                            known = jnp.where(name >= n * LANES, other, known)
                        is_open = value > known
                        found.append(
                            (
                                jnp.where(is_open, value, FLOOR),
                                name,
                                jnp.where(is_open, 1.0, 0.0),
                            )
                        )
                    while len(found) > 1:
                        paired = [merge(a, b) for a, b in zip(found[::2], found[1::2])]
                        found = paired + found[2 * len(paired) :]
                    merged.append(found[0])
                return tuple(merged)

            floor = jnp.full((8, LANES), FLOOR, jnp.float32)
            init = ((floor, jnp.zeros((8, LANES), jnp.int32), tiny),) * (2 * tiles)
            state = lax.fori_loop(0, rows // (8 * SCAN_ROWS), per_rows, init)
            count = functools.reduce(jnp.maximum, [part[2] for part in state])
            most = jnp.max(count)

            @pl.when(most > 0.0)
            def _():
                raise_tops([part[0] for part in state], [part[1] for part in state])

            return most

        lax.while_loop(lambda most: most > 1.0, scan, jnp.float32(2.0))
        out_ref[...] = tops()

    return pl.pallas_call(
        body,
        out_shape=(whole((rows, lon_count), jnp.bfloat16), whole((1, storm_count), jnp.float32)),
        in_specs=[IN_VMEM] * 4,
        out_specs=(IN_VMEM, IN_VMEM),
        scratch_shapes=[
            pltpu.VMEM((ranks, groups * band_rows * GROUP, columns), jnp.float32),
            pltpu.VMEM((2 * wave_tiles, rows, LANES), jnp.float32),
            pltpu.VMEM((tiles, rows, LANES), jnp.float32),
            pltpu.VMEM((rows, LANES), jnp.int32),
            pltpu.VMEM((storm_count, LANES), jnp.float32),
        ],
        compiler_params=params(24),
    )(early, late, synthesis, labels)


def after(x, *others):
    return lax.optimization_barrier((x, *others))[0]


def local(vorticity, lat_order, storm_labels, storm_owner):
    field_count, lat_rows, lon_count = vorticity.shape
    lat_count = lat_order.shape[0]
    halves = lax.axis_size("half")
    ranks = lax.axis_size("rest")
    half_index = lax.axis_index("half")
    rank = lax.axis_index("rest")
    band_rows = storm_labels.shape[1]
    storm_count = storm_owner.shape[0]
    slots = MW // ranks
    chunks = slots // GROUP
    columns = 2 * field_count
    out_half = OUT_LAT // halves

    calls = [[16], [8, 8]] if slots == 32 else [[slots // 2], [slots // 2]]
    full_table = fourier_table(lon_count).reshape(lon_count, slots, ranks, 2)
    coefficients = []
    first = 0
    for part_slots in calls:
        pieces = []
        base = first
        for n in part_slots:
            pieces.append(full_table[:, base : base + n].transpose(0, 2, 1, 3).reshape(lon_count, -1, 2))
            base += n
        table = np.concatenate(pieces, axis=1).transpose(0, 2, 1).reshape(lon_count, -1)
        table = jnp.asarray(table.astype(jnp.bfloat16))
        coefficients += fourier(vorticity, table, ranks, part_slots)
        first = base
    stages = [n // GROUP for part_slots in calls for n in part_slots]
    group_count = slots // GROUP

    half_rows = ranks * lat_rows
    own_order = lax.dynamic_slice_in_dim(lat_order, half_index * half_rows, half_rows)
    colatitude = math.pi * (4.0 * own_order.astype(jnp.float32) + 3.0) / (4.0 * lat_count + 2.0)
    weights = math.pi / lat_count * jnp.sin(colatitude)
    band_index = jnp.arange(OUT_LAT, dtype=jnp.int32)
    band_index = ((band_index + half_index * out_half) % OUT_LAT).astype(jnp.float32)
    latitude = ((OUT_LAT - 1) / 2.0 - band_index) * (360.0 / OUT_LON) * (math.pi / 180.0)
    sine_values = jnp.concatenate([jnp.cos(latitude), jnp.sin(colatitude)])
    cosines = jnp.concatenate([jnp.sin(latitude), jnp.cos(colatitude)])
    orders = jnp.arange(slots, dtype=jnp.int32) * ranks + rank
    start_logs = jnp.asarray(diagonal_logs().reshape(slots, ranks))
    start_logs = lax.dynamic_slice_in_dim(start_logs, rank, 1, axis=1)
    orders = orders.astype(jnp.float32)[:, None]
    start = jnp.exp(start_logs + orders * jnp.log(sine_values)[None, :])
    def kernel(group, token):
        ordered = start if token is None else after(start, token)
        return kernel_table(
            orders[group * GROUP : (group + 1) * GROUP],
            ordered[group * GROUP : (group + 1) * GROUP],
            cosines[None, :],
            weights[None, :],
            OUT_LAT,
            MW - group * GROUP * ranks,
            out_half if group == group_count - 1 else 0,
        )

    def exchange(block):
        return lax.all_to_all(block, "rest", split_axis=0, concat_axis=0, tiled=True)

    def swapped(block):
        return lax.ppermute(block, "half", [(0, 1), (1, 0)])

    begins = [sum(stages[:i]) for i in range(len(stages) + 1)]
    last_stage = len(stages) - 1
    received = exchange(coefficients[0])
    tables = [kernel(0, coefficients[-1][0, 0, 0, :1])]
    cover = [coefficients[-1], *[part for table in tables for part in table]]
    swaps = []
    bands = []
    for i, count in enumerate(stages):
        received = after(received, *cover)
        if i == 1 and i < last_stage:
            received = after(received, swaps[0])
        following = None
        if i < last_stage:
            following = exchange(after(coefficients[i + 1], received))
        for g in range(begins[i], begins[i + 1]):
            if g == group_count - 1:
                own, other = spectral_part(tables[g][0], received, ranks)
                band = spectral_band(tables[g][1], own, swapped(other), ranks)
            else:
                own, other = apply_table(tables[g][0], received, (g - begins[i]) * GROUP)
                swaps.append(swapped(other))
                band = (own + swaps[-1].astype(jnp.float32)).astype(jnp.bfloat16)
            bands.append(band.reshape(ranks, band_rows * GROUP, columns))
            if i == 0 and g + 1 < stages[0]:
                tables.append(kernel(g + 1, other[0, :1]))
        if i == 0:
            later = [kernel(g, other[0, :1]) for g in range(stages[0], group_count)]
            tables += later
            cover = [other, *[part for table in later for part in table]]
        else:
            cover = [other, *bands]
        last_received, received = received, following

    early = exchange(after(jnp.concatenate(bands[:-1], axis=1), last_received))
    late = exchange(after(bands[-1], early))
    synthesis = synthesis_table(OUT_LON).reshape(group_count, GROUP, ranks, 2, OUT_LON)
    synthesis = synthesis.transpose(3, 2, 0, 1, 4).reshape(2 * MW, OUT_LON)
    synthesis = np.pad(synthesis, ((0, 0), (0, -OUT_LON % LANES)))
    filtered, local_peaks = grid_maxima(
        early,
        late,
        jnp.asarray(synthesis.astype(jnp.bfloat16)),
        storm_labels.reshape(field_count * band_rows, OUT_LON),
        band_rows,
        field_count,
        storm_count,
    )
    filtered = filtered.reshape(field_count, band_rows, OUT_LON)
    local_peaks = local_peaks[0]
    slot_ids = jnp.arange(storm_count, dtype=jnp.int32)
    by_slot = jnp.max(
        jnp.where(storm_owner[:, None] == slot_ids[None, :], local_peaks[:, None], FLOOR), axis=0
    )
    spec_count = halves * ranks
    shares = lax.all_to_all(
        by_slot.reshape(spec_count, storm_count // spec_count),
        ("half", "rest"),
        split_axis=0,
        concat_axis=0,
        tiled=True,
    )
    return (filtered, jnp.max(shares, axis=0))


def solution(mesh):
    groups = mesh.shape["grp"]
    spec_count = mesh.shape["spec"]
    split = Mesh(
        mesh.devices.reshape(groups, 2, spec_count // 2), axis_names=("grp", "half", "rest")
    )
    both = ("half", "rest")
    return jax.shard_map(
        local,
        mesh=split,
        in_specs=(P("grp", both, None), P(), P("grp", both, None), P("grp")),
        out_specs=(P("grp", both, None), P(("grp", "half", "rest"))),
        check_vma=False,
    )
```
